32 devices in a mesh: ens: 2 (over x), tile: 16 (over z, y, core).
Axes of the slice: x: 2, y: 2, z: 4, core: 2. Of those that a mesh axis runs over, the one named last changes fastest.
Arguments:
- final_adjoint: float32 [320, 32, 1024], P('ens', 'tile'), parts along dimension 0, may hold values from -0.5 to 1.5
- first_density: float32 [320, 32, 1024], P('ens', 'tile'), parts along dimension 0, may hold values from 0.05 to 2
- second_density: float32 [320, 32, 1024], P('ens', 'tile'), parts along dimension 0, may hold values from 0.05 to 2
- forage: float32 [4, 6, 32, 1024], P('ens', None, 'tile'), parts along dimension 0, may hold values from 5 to 50
- preference: float32 [32, 6], P('ens'), parts along dimension 0, may hold values from 0.02 to 0.3
- base_mortality: float32 [160], replicated, may hold values from 0.01 to 0.5
- age_class: int32 [160], replicated, may hold values from 0 to 15, never falling along the last dimension, each value on 1 to 20 neighbouring positions
- land_mask: int32 [32, 1024], P('tile'), may hold values 0 or 1
- east_velocity: float32 [32, 1024], P('tile'), may hold values from -0.1 to 0.1
- north_velocity: float32 [32, 1024], P('tile'), may hold values from -0.1 to 0.1
Outputs:
- initial_adjoint: float32 [320, 32, 1024], P('ens', 'tile'), parts along dimension 0
- forage_sensitivity: float32 [4, 6, 32, 1024], P('ens', None, 'tile'), parts along dimension 0
- preference_gradient: float32 [32, 6], P('ens'), parts along dimension 0
The draws below stay inside these ranges and needn't reach their ends.
There are 2 independent parts, one for each index of `ens`. The reference program is written for one: setup_inputs(seed, part) draws one part's arguments, and reference() takes and returns one part's arrays. A program takes and returns all parts, laid end to end along the dimension named above; an argument that names none is the same for every part. Nothing has to cross between parts.
Inputs may be any that keep to these rules, and one draw needn't show every extreme that they name: `age_class`: never falls along the cohorts; every class holds 1 to 20 cohorts, one exactly that many.
All inputs are finite; a program needn't handle non-finite values. No bound on the sum of `land_mask` on one device may be relied on, other than what follows from the above.
Results may differ from the reference program's by a relative error of at most 0.00011.
Values sent between devices are 32-bit elements; how exact they have to be, the bound alone decides.
A program may use at most 64 MiB of HBM per device.

```python
import math
import jax
import jax.numpy as jnp
import numpy as np
from jax import lax

COH = 160
NX = 1024
FORAGE = 6
CLASSES = 16
SUBSTEPS = 4
MONTHS = 2
NY = 32


def touch_ends(result, stream_key, smallest, high):
    longest = result.shape.index(max(result.shape))
    spots = []
    for shift in (0, 1):
        where = [jax.random.randint(jax.random.fold_in(stream_key, axis), (), 0, length) for axis, length in enumerate(result.shape)]
        where[longest] = (where[longest] + shift) % result.shape[longest]
        spots.append(tuple(where))
    return result.at[spots[0]].set(smallest).at[spots[1]].set(high)


def block_levels(key, shape, pieces, smallest, largest):
    def one(position, parts):
        steps = jax.random.uniform(jax.random.fold_in(jax.random.fold_in(key, 6), position), (parts,), jnp.float32, smallest / len(pieces), largest / len(pieces))
        return jnp.repeat(jnp.exp(steps), shape[position] // parts).reshape((-1,) + (1,) * (len(shape) - position - 1))

    gain = one(*pieces[0])
    for cut in pieces[1:]:
        gain = gain * one(*cut)
    return gain


def length_profile(count, total, reach, lean):
    loads = [(1 << 20) // math.isqrt(standing ** lean) + 1 for standing in range(2, count + 1)]
    surplus, counts = total - reach - (count - 1), [1] * (count - 1)
    while surplus > 0:
        movable = [i for i in range(count - 1) if counts[i] < reach]
        mass, remaining = sum([loads[i] for i in movable]), surplus
        for i in movable:
            addition = min(reach - counts[i], max(1, remaining * loads[i] // mass), surplus)
            counts[i] = counts[i] + addition
            surplus = surplus - addition
    return np.array([reach] + counts)


def uneven_parts(stream_key, number_of, total, bound, slope):
    if number_of == 2:
        one = jax.random.randint(stream_key, (), max(1, total - bound), min(bound, total - 1) + 1)
        return jnp.stack([one, total - one])
    lengths = jnp.asarray(length_profile(number_of, total, bound, slope), jnp.int32)
    twos = (number_of - 1) // 2
    source_of, sink = lengths[1:1 + 2 * twos:2], lengths[2:2 + 2 * twos:2]
    slack = jnp.minimum(source_of - 1, bound - sink)
    shifted = jax.random.randint(jax.random.fold_in(stream_key, 1), (twos,), 0, 1 << 20) % (slack + 1)
    lengths = lengths.at[1:1 + 2 * twos:2].set(source_of - shifted).at[2:2 + 2 * twos:2].set(sink + shifted)
    return lengths[jax.random.permutation(jax.random.fold_in(stream_key, 2), number_of)]


def setup_inputs(seed: int = 0, part: int = 0) -> dict:
    splits = jax.random.split(jax.random.key(seed), 11)
    own_keys = jax.random.split(jax.random.fold_in(splits[10], part), 11)
    return {
        "final_adjoint": jnp.clip(-0.5 + 2.0 * jax.random.uniform(own_keys[0], (COH, NY, NX), jnp.float32) ** block_levels(own_keys[0], (COH, NY, NX), ((1, 16),), -0.2, 0.2), -0.5, 1.5),
        "first_density": jnp.clip(jnp.exp(math.log(2.0) - 3.6888794 * jax.random.uniform(own_keys[1], (COH, NY, NX), jnp.float32) ** block_levels(own_keys[1], (COH, NY, NX), ((1, 16),), -0.2, 0.2)), 0.05, 2.0),
        "second_density": jnp.clip(jnp.exp(math.log(2.0) - 3.6888794 * jax.random.uniform(own_keys[2], (COH, NY, NX), jnp.float32) ** block_levels(own_keys[2], (COH, NY, NX), ((1, 16),), -0.2, 0.2)), 0.05, 2.0),
        "forage": jnp.clip(jnp.exp(math.log(50.0) - 2.3025851 * jax.random.uniform(own_keys[3], (MONTHS, FORAGE, NY, NX), jnp.float32) ** block_levels(own_keys[3], (MONTHS, FORAGE, NY, NX), ((2, 16),), -0.2, 0.2)), 5.0, 50.0),
        "preference": jnp.clip(jax.random.uniform(own_keys[4], (CLASSES, FORAGE), jnp.float32, 0.02, 0.3), 0.02, 0.3),
        "base_mortality": jnp.clip(jnp.exp(jax.random.uniform(splits[5], (COH,), jnp.float32, math.log(0.01), math.log(0.5))), 0.01, 0.5),
        "age_class": jnp.searchsorted(jnp.cumsum(uneven_parts(splits[6], CLASSES, COH, COH // CLASSES * 2, 1)), jnp.arange(COH), side="right").astype(jnp.int32),
        "land_mask": touch_ends((jax.random.randint(splits[7], (NY, NX), 0, 4) < 3).astype(jnp.int32), jax.random.fold_in(splits[7], 1), 0, 1),
        "east_velocity": jnp.clip(jax.random.uniform(splits[8], (NY, NX), jnp.float32, -0.1, 0.1) * block_levels(splits[8], (NY, NX), ((0, 16),), -0.4, 0.0), -0.1, 0.1),
        "north_velocity": jnp.clip(jax.random.uniform(splits[9], (NY, NX), jnp.float32, -0.1, 0.1) * block_levels(splits[9], (NY, NX), ((0, 16),), -0.4, 0.0), -0.1, 0.1),
    }


HIGH = lax.Precision.HIGHEST


def make_rates(land_mask, east_velocity, north_velocity):
    mask = land_mask.astype(jnp.float32)
    padded = jnp.pad(mask, ((1, 1), (0, 0)))
    north_mask = padded[:-2]
    south_mask = padded[2:]
    east_mask = jnp.roll(mask, -1, axis=1)
    west_mask = jnp.roll(mask, 1, axis=1)
    rate_n = mask * north_mask * (0.1 + jnp.maximum(north_velocity, 0.0))
    rate_s = mask * south_mask * (0.1 + jnp.maximum(-north_velocity, 0.0))
    rate_e = mask * east_mask * (0.1 + jnp.maximum(east_velocity, 0.0))
    rate_w = mask * west_mask * (0.1 + jnp.maximum(-east_velocity, 0.0))
    keep = 1.0 - rate_n - rate_s - rate_e - rate_w
    return keep, rate_n, rate_s, rate_e, rate_w


def transpose_step(field, rates):
    keep, rate_n, rate_s, rate_e, rate_w = rates
    padded = jnp.pad(field, ((0, 0), (1, 1), (0, 0)))
    return (keep * field + rate_n * padded[:, :-2] + rate_s * padded[:, 2:]
            + rate_e * jnp.roll(field, -1, axis=2) + rate_w * jnp.roll(field, 1, axis=2))


def month_adjoint(incoming, density, food, pref_rows, base_mortality, rates, onehot):
    carried = incoming
    for step in range(SUBSTEPS):
        carried = transpose_step(carried, rates)
    cohorts = carried.shape[0]
    aged = jnp.concatenate([carried[1:], carried[cohorts - 1:]], axis=0).reshape(cohorts, -1)
    dens = density.reshape(cohorts, -1)
    feed = food.reshape(food.shape[0], -1)
    demand = jnp.dot(pref_rows.T, dens, precision=HIGH)
    total = feed + demand
    short = demand / total
    survival = jnp.exp(-(base_mortality[:, None] + jnp.dot(pref_rows, short, precision=HIGH)))
    grown = survival * dens
    adj_mort = -aged * grown
    adj_ratio = -jnp.dot(pref_rows.T, adj_mort, precision=HIGH)
    squared = total * total
    adj_demand = -adj_ratio * feed / squared
    sensitivity = adj_ratio * demand * feed / squared
    outgoing = aged * survival + jnp.dot(pref_rows, adj_demand, precision=HIGH)
    cohort_grad = jnp.dot(adj_mort, short.T, precision=HIGH) + jnp.dot(dens, adj_demand.T, precision=HIGH)
    class_grad = jnp.dot(onehot, cohort_grad, precision=HIGH)
    return outgoing.reshape(density.shape), sensitivity.reshape(food.shape), class_grad


def reference(final_adjoint, first_density, second_density, forage, preference, base_mortality,
              age_class, land_mask, east_velocity, north_velocity):
    classes = preference.shape[0]
    onehot = (age_class[None, :] == jnp.arange(classes, dtype=jnp.int32)[:, None]).astype(jnp.float32)
    pref_rows = jnp.dot(onehot.T, preference, precision=HIGH)
    rates = make_rates(land_mask, east_velocity, north_velocity)
    middle, sens_two, grad_two = month_adjoint(final_adjoint, second_density, forage[1], pref_rows,
                                               base_mortality, rates, onehot)
    initial, sens_one, grad_one = month_adjoint(middle, first_density, forage[0], pref_rows,
                                                base_mortality, rates, onehot)
    cells = land_mask.shape[0] * land_mask.shape[1]
    return initial, jnp.stack([sens_one, sens_two], axis=0), (grad_one + grad_two) / cells
```

```python
import jax
import jax.numpy as jnp
from jax import lax
from jax.experimental import pallas as pl
from jax.experimental.pallas import tpu as pltpu
from jax.sharding import PartitionSpec as P

SUBSTEPS = 4
LANES = 128
MESH = pl.DeviceIdType.MESH


def cuts(total, parts):
    size = max(1, total // parts)
    starts = [i * size for i in range(parts)]
    return [(s, (size if i < parts - 1 else total - s)) for i, s in enumerate(starts)]


def kernel(
    dims,
    pref,
    base,
    lead,
    dens1,
    dens2,
    food,
    fields,
    out,
    sens,
    grad,
    wide2,
    wide1,
    done2,
    done1,
    aged2,
    aged1,
    strip,
    rates,
    short_all,
    adem_all,
    short1,
    feed_sq,
    surv,
    lsend,
    lrecv,
    zsend,
    zrecv,
    osend,
    orecv,
    z1send,
    z1recv,
    o1send,
    o1recv,
    fsend,
    frecv,
    hsend,
    hrecv,
    ssend,
    srecv,
    asend,
    arecv,
    own_sem,
):
    tiles, group, cohorts, quarter, forage, chunks = dims
    half = group // 2
    blocks = food.shape[2]
    me = lax.axis_index("tile")
    q = lax.rem(me, group)
    first = me - q
    has_prev = me >= group
    has_next = me < tiles - group

    def peer(o):
        return first + lax.rem(q + o, group)

    def source(o):
        return lax.rem(q + group - o, group)

    barrier = pltpu.get_barrier_semaphore()
    for o in range(1, group):
        pl.semaphore_signal(barrier, inc=1, device_id={"tile": peer(o)}, device_id_type=MESH)

    @pl.when(has_prev)
    def _():
        pl.semaphore_signal(barrier, inc=1, device_id={"tile": me - group}, device_id_type=MESH)

    @pl.when(has_next)
    def _():
        pl.semaphore_signal(barrier, inc=1, device_id={"tile": me + group}, device_id_type=MESH)

    sides = has_prev.astype(jnp.int32) + has_next.astype(jnp.int32)
    pl.semaphore_wait(barrier, group - 1 + sides)

    def remote(src, dst, ssem, rsem, target):
        return pltpu.make_async_remote_copy(
            src_ref=src, dst_ref=dst, send_sem=ssem, recv_sem=rsem,
            device_id={"tile": target}, device_id_type=MESH,
        )

    def gather_copy(buf, ssem, rsem, o):
        return remote(buf.at[q], buf.at[q], ssem.at[o], rsem.at[o], peer(o))

    def gather_wait(buf, ssem, rsem, o):
        spot = buf.at[source(o)]
        remote(spot, spot, ssem.at[o], rsem.at[o], peer(o)).wait_recv()

    def halo(buf, lo, size, ssem, rsem, c):
        down = remote(
            buf.at[pl.ds(group, half), pl.ds(lo, size)], buf.at[pl.ds(0, half), pl.ds(lo, size)],
            ssem.at[0, c], rsem.at[0, c], me + group,
        )
        up = remote(
            buf.at[pl.ds(half, half), pl.ds(lo, size)],
            buf.at[pl.ds(group + half, half), pl.ds(lo, size)],
            ssem.at[1, c], rsem.at[1, c], me - group,
        )
        return down, up

    def halo_start(*args):
        down, up = halo(*args)

        @pl.when(has_next)
        def _():
            down.start()

        @pl.when(has_prev)
        def _():
            up.start()

    def halo_wait(*args):
        down, up = halo(*args)

        @pl.when(has_prev)
        def _():
            down.wait_recv()

        @pl.when(has_next)
        def _():
            up.wait_recv()

    def halo_sent(*args):
        down, up = halo(*args)

        @pl.when(has_next)
        def _():
            down.wait_send()

        @pl.when(has_prev)
        def _():
            up.wait_send()

    own_field = pltpu.make_async_copy(fields, strip.at[half + q], own_sem.at[0])
    own_field.start()
    for o in range(1, group):
        remote(fields, strip.at[half + q], fsend.at[o], frecv.at[o], peer(o)).start()

    lead_cuts = cuts(quarter + 1, chunks)
    part_cuts = cuts(quarter, chunks)

    def lead_copy(o, c):
        lo, size = lead_cuts[c]
        to = lax.rem(q + o, group)
        return remote(
            lead.at[pl.ds(to * quarter + lo, size)], wide2.at[half + q, pl.ds(lo, size)],
            lsend.at[o, c], lrecv.at[o, c], peer(o),
        )

    own_lead = pltpu.make_async_copy(
        lead.at[pl.ds(q * quarter, quarter + 1)], wide2.at[half + q], own_sem.at[1]
    )
    own_lead.start()
    for c in range(chunks):
        for o in range(1, group):
            lead_copy(o, c).start()

    @pl.when(jnp.logical_not(has_prev))
    def _():
        strip[0:half] = jnp.zeros((half,) + strip.shape[1:], jnp.float32)
        wide2[0:half] = jnp.zeros((half,) + wide2.shape[1:], jnp.float32)
        wide1[0:half] = jnp.zeros((half,) + wide1.shape[1:], jnp.float32)

    @pl.when(jnp.logical_not(has_next))
    def _():
        strip[group + half :] = jnp.zeros((half,) + strip.shape[1:], jnp.float32)
        wide2[group + half :] = jnp.zeros((half,) + wide2.shape[1:], jnp.float32)
        wide1[group + half :] = jnp.zeros((half,) + wide1.shape[1:], jnp.float32)

    zero = jnp.zeros((blocks, LANES), jnp.float32)

    def demands(dens):
        def step(a, sums):
            n = dens[a]
            return tuple(sums[k] + pref[a * forage + k] * n for k in range(forage))

        return lax.fori_loop(0, cohorts, step, (zero,) * forage, unroll=4)

    def prepare(month, dens, short_store):
        sums = demands(dens)
        for k in range(forage):
            feed = food[month, k]
            total = feed + sums[k]
            short_store(k, sums[k] / total)
            feed_sq[month, k] = feed / (total * total)
            feed_sq[2 + month, k] = sums[k]

    def store_two(k, value):
        short_all[q, k] = value

    def store_one(k, value):
        short1[k] = value

    prepare(1, dens2, store_two)
    for o in range(1, group):
        gather_copy(short_all, ssend, srecv, o).start()

    own_field.wait()
    for o in range(1, group):
        spot = strip.at[half + source(o)]
        remote(spot, spot, fsend.at[o], frecv.at[o], peer(o)).wait_recv()
    halo_start(strip, 0, 3, hsend, hrecv, 0)
    own_lead.wait()
    lane = lax.broadcasted_iota(jnp.int32, (blocks, LANES), 1)
    odd = lax.rem(lax.broadcasted_iota(jnp.int32, (blocks, LANES), 0), 2) == 1
    last_lane = lane == LANES - 1
    first_lane = lane == 0

    def east_of(x):
        near = pltpu.roll(x, LANES - 1, 1)
        return jnp.where(last_lane, pltpu.roll(near, blocks - 2, 0), near)

    def west_of(x):
        near = pltpu.roll(x, 1, 1)
        return jnp.where(first_lane, pltpu.roll(near, 2, 0), near)

    def vertical(slots, s):
        above = slots[s - 1] if s > 0 and slots[s - 1] is not None else zero
        below = slots[s + 1] if s + 1 < len(slots) and slots[s + 1] is not None else zero
        north = jnp.where(odd, pltpu.roll(slots[s], 1, 0), pltpu.roll(above, blocks - 1, 0))
        south = jnp.where(odd, pltpu.roll(below, 1, 0), pltpu.roll(slots[s], blocks - 1, 0))
        return north, south

    prepare(0, dens1, store_one)

    def lead_wait(c):
        lo, size = lead_cuts[c]
        for o in range(1, group):
            spot = wide2.at[half + source(o), pl.ds(lo, size)]
            remote(spot, spot, lsend.at[o, c], lrecv.at[o, c], peer(o)).wait_recv()

    lead_wait(0)
    halo_start(wide2, *lead_cuts[0], zsend, zrecv, 0)
    halo_wait(strip, 0, 3, hsend, hrecv, 0)
    masks = [strip[s, 0] for s in range(2 * group)]
    for s in range(2 * group):
        mask, east, north = masks[s], strip[s, 1], strip[s, 2]
        mask_n, mask_s = vertical(masks, s)
        rate_n = mask * mask_n * (0.1 + jnp.maximum(north, 0.0))
        rate_s = mask * mask_s * (0.1 + jnp.maximum(-north, 0.0))
        rate_e = mask * east_of(mask) * (0.1 + jnp.maximum(east, 0.0))
        rate_w = mask * west_of(mask) * (0.1 + jnp.maximum(-east, 0.0))
        rates[s, 0] = 1.0 - rate_n - rate_s - rate_e - rate_w
        rates[s, 1] = rate_n
        rates[s, 2] = rate_s
        rates[s, 3] = rate_e
        rates[s, 4] = rate_w

    def transport(wide, done, lo, size):
        def body(i, carry):
            slots = [wide[s, i] for s in range(2 * group)]
            for step in range(SUBSTEPS):
                margin = (step + 1) // 2
                new = [None] * (2 * group)
                for s in range(margin, 2 * group - margin):
                    north, south = vertical(slots, s)
                    new[s] = (
                        rates[s, 0] * slots[s]
                        + rates[s, 1] * north
                        + rates[s, 2] * south
                        + rates[s, 3] * east_of(slots[s])
                        + rates[s, 4] * west_of(slots[s])
                    )
                slots = new
            for s in range(group):
                done[s, i] = slots[half + s]
            return carry

        lax.fori_loop(lo, lo + size, body, 0)

    def out_copy(done, aged, o, c, ssem, rsem):
        lo, size = part_cuts[c]
        return remote(
            done.at[lax.rem(q + o, group), pl.ds(lo, size)],
            aged.at[pl.ds(q * quarter + lo, size)], ssem.at[o, c], rsem.at[o, c], peer(o),
        )

    def out_own(done, aged, c, sem):
        lo, size = part_cuts[c]
        return pltpu.make_async_copy(
            done.at[q, pl.ds(lo, size)], aged.at[pl.ds(q * quarter + lo, size)], sem.at[0, c]
        )

    def out_wait(aged, o, c, ssem, rsem):
        lo, size = part_cuts[c]
        spot = aged.at[pl.ds(source(o) * quarter + lo, size)]
        remote(spot, spot, ssem.at[o, c], rsem.at[o, c], peer(o)).wait_recv()

    for c in range(chunks):
        if c + 1 < chunks:
            lead_wait(c + 1)
            halo_start(wide2, *lead_cuts[c + 1], zsend, zrecv, c + 1)
        halo_wait(wide2, *lead_cuts[c], zsend, zrecv, c)
        transport(wide2, done2, *lead_cuts[c])
        for o in range(1, group):
            out_copy(done2, aged2, o, c, osend, orecv).start()
        out_own(done2, aged2, c, orecv).start()

    def ratio_part(lo, size, aged, dens, short, sums):
        def step(a, sums):
            level = base[a]
            hunger = [pref[a * forage + k] for k in range(forage)]
            for k in range(forage):
                level = level + hunger[k] * short[k]
            kept = jnp.exp(-level)
            surv[a] = kept
            dying = aged[a] * kept * dens[a]
            return tuple(sums[k] + hunger[k] * dying for k in range(forage))

        for part in range(group):
            start = part * quarter + lo
            sums = lax.fori_loop(start, start + size, step, sums, unroll=2)
        return sums

    def finish(month, ratio):
        adem = []
        for k in range(forage):
            adem.append(-ratio[k] * feed_sq[month, k])
            sens[month, k] = ratio[k] * feed_sq[2 + month, k] * feed_sq[month, k]
        return adem

    def slopes(aged, dens, short, adem, add):
        def step(a, carry):
            n = dens[a]
            kept = surv[a]
            dying = aged[a] * kept * n
            rows = []
            for k in range(forage):
                both = n * adem[k] - dying * short[k]
                rows.append(jnp.sum(both, axis=0, keepdims=True))
            rows = jnp.concatenate(rows, axis=0)
            if add:
                rows = rows + grad[a]
                total = aged[a] * kept
                for k in range(forage):
                    total = total + pref[a * forage + k] * adem[k]
                out[a] = total
            grad[a] = rows
            return carry

        lax.fori_loop(0, cohorts, step, 0, unroll=2)

    short2 = [short_all[q, k] for k in range(forage)]
    ratio = (zero,) * forage
    for c in range(chunks):
        for o in range(1, group):
            out_wait(aged2, o, c, osend, orecv)
        out_own(done2, aged2, c, orecv).wait()
        ratio = ratio_part(*part_cuts[c], aged2, dens2, short2, ratio)
    adem2 = finish(1, ratio)
    for k in range(forage):
        adem_all[q, k] = adem2[k]
    for o in range(1, group):
        gather_copy(adem_all, asend, arecv, o).start()
    for o in range(1, group):
        gather_wait(short_all, ssend, srecv, o)
    for o in range(1, group):
        gather_wait(adem_all, asend, arecv, o)

    for c in range(chunks):
        lo, size = part_cuts[c]

        def middle(i, carry):
            a = jnp.minimum(q * quarter + i + 1, cohorts - 1)
            hunger = [pref[a * forage + k] for k in range(forage)]
            for s in range(group):
                level = base[a]
                add = zero
                for k in range(forage):
                    level = level + hunger[k] * short_all[s, k]
                    add = add + hunger[k] * adem_all[s, k]
                wide1[half + s, i] = done2[s, i + 1] * jnp.exp(-level) + add
            return carry

        lax.fori_loop(lo, lo + size, middle, 0)
        halo_start(wide1, lo, size, z1send, z1recv, c)
    slopes(aged2, dens2, short2, adem2, False)

    for c in range(chunks):
        halo_wait(wide1, *part_cuts[c], z1send, z1recv, c)
        transport(wide1, done1, *part_cuts[c])
        for o in range(1, group):
            out_copy(done1, aged1, o, c, o1send, o1recv).start()
        out_own(done1, aged1, c, o1recv).start()

    short_one = [short1[k] for k in range(forage)]
    ratio = (zero,) * forage
    for c in range(chunks):
        for o in range(1, group):
            out_wait(aged1, o, c, o1send, o1recv)
        out_own(done1, aged1, c, o1recv).wait()
        ratio = ratio_part(*part_cuts[c], aged1, dens1, short_one, ratio)
    adem1 = finish(0, ratio)
    slopes(aged1, dens1, short_one, adem1, True)

    for o in range(1, group):
        remote(fields, strip.at[half + q], fsend.at[o], frecv.at[o], peer(o)).wait_send()
        gather_copy(short_all, ssend, srecv, o).wait_send()
        gather_copy(adem_all, asend, arecv, o).wait_send()
        for c in range(chunks):
            lead_copy(o, c).wait_send()
            out_copy(done2, aged2, o, c, osend, orecv).wait_send()
            out_copy(done1, aged1, o, c, o1send, o1recv).wait_send()
    halo_sent(strip, 0, 3, hsend, hrecv, 0)
    for c in range(chunks):
        halo_sent(wide2, *lead_cuts[c], zsend, zrecv, c)
        halo_sent(wide1, *part_cuts[c], z1send, z1recv, c)


def blocked(x):
    rows, columns = x.shape[-2:]
    head = x.shape[:-2]
    n = len(head)
    y = x.reshape(head + (rows, columns // LANES, LANES))
    y = jnp.swapaxes(y, n, n + 1)
    return y.reshape(head + (rows * columns // LANES, LANES))


def unblocked(x, rows):
    head = x.shape[:-2]
    n = len(head)
    y = x.reshape(head + (x.shape[-2] // rows, rows, LANES))
    y = jnp.swapaxes(y, n, n + 1)
    return y.reshape(head + (rows, -1))


def shards(
    final_adjoint,
    first_density,
    second_density,
    forage,
    preference,
    base_mortality,
    age_class,
    land_mask,
    east_velocity,
    north_velocity,
):
    classes, groups = preference.shape
    cohorts, rows, columns = final_adjoint.shape
    tiles = lax.axis_size("tile")
    group = 2 * SUBSTEPS // rows
    quarter = cohorts // group
    chunks = 5
    blocks = rows * columns // LANES
    pref_rows = preference[age_class]
    fields = blocked(jnp.stack([land_mask.astype(jnp.float32), east_velocity, north_velocity]))
    incoming = blocked(final_adjoint)
    tail = incoming[cohorts - 1 :]
    lead = jnp.concatenate([incoming[1:], tail, tail], axis=0)
    f32 = jnp.float32
    dma = pltpu.SemaphoreType.DMA
    vmem = pl.BlockSpec(memory_space=pltpu.VMEM)
    smem = pl.BlockSpec(memory_space=pltpu.SMEM)
    dims = (tiles, group, cohorts, quarter, groups, chunks)
    cell = (blocks, LANES)
    pair = [dma((group, chunks)), dma((group, chunks))]
    hop = [dma((2, chunks)), dma((2, chunks))]
    one = [dma((group,)), dma((group,))]

    def body(*refs):
        kernel(dims, *refs)

    out, sens, grad = pl.pallas_call(
        body,
        out_shape=(
            jax.ShapeDtypeStruct((cohorts,) + cell, f32),
            jax.ShapeDtypeStruct((2, groups) + cell, f32),
            jax.ShapeDtypeStruct((cohorts, groups, LANES), f32),
        ),
        in_specs=[smem, smem] + [vmem] * 5,
        out_specs=(vmem, vmem, vmem),
        scratch_shapes=[
            pltpu.VMEM((2 * group, quarter + 1) + cell, f32),
            pltpu.VMEM((2 * group, quarter) + cell, f32),
            pltpu.VMEM((group, quarter + 1) + cell, f32),
            pltpu.VMEM((group, quarter) + cell, f32),
            pltpu.VMEM((cohorts,) + cell, f32),
            pltpu.VMEM((cohorts,) + cell, f32),
            pltpu.VMEM((2 * group, 3) + cell, f32),
            pltpu.VMEM((2 * group, 5) + cell, f32),
            pltpu.VMEM((group, groups) + cell, f32),
            pltpu.VMEM((group, groups) + cell, f32),
            pltpu.VMEM((groups,) + cell, f32),
            pltpu.VMEM((4, groups) + cell, f32),
            pltpu.VMEM((cohorts,) + cell, f32),
        ]
        + pair + hop + pair + hop + pair + one
        + [dma((2, 1)), dma((2, 1))] + one + one + [dma((2,))],
        compiler_params=pltpu.CompilerParams(
            collective_id=0, has_side_effects=True, vmem_limit_bytes=48 * 1024 * 1024
        ),
        name="adjoint",
    )(
        pref_rows.reshape(-1),
        base_mortality,
        lead,
        blocked(first_density),
        blocked(second_density),
        blocked(forage),
        fields,
    )
    onehot = (age_class[None, :] == jnp.arange(classes, dtype=jnp.int32)[:, None]).astype(f32)
    local = jnp.dot(onehot, jnp.sum(grad, axis=2), precision=lax.Precision.HIGHEST)
    cells = land_mask.shape[0] * tiles * land_mask.shape[1]
    summed = lax.psum(local, "tile") / cells
    return (unblocked(out, rows), unblocked(sens, rows), summed)


def solution(mesh):
    in_specs = (
        P("ens", "tile", None),
        P("ens", "tile", None),
        P("ens", "tile", None),
        P("ens", None, "tile", None),
        P("ens", None),
        P(),
        P(),
        P("tile", None),
        P("tile", None),
        P("tile", None),
    )
    out_specs = (P("ens", "tile", None), P("ens", None, "tile", None), P("ens", None))
    return jax.shard_map(shards, mesh=mesh, in_specs=in_specs, out_specs=out_specs, check_vma=False)
```

```python
import jax
import jax.numpy as jnp
from jax import lax
from jax.experimental import pallas as pl
from jax.experimental.pallas import tpu as pltpu
from jax.sharding import PartitionSpec as P

SUBSTEPS = 4
LANES = 128
MESH = pl.DeviceIdType.MESH


def cuts(total, parts):
    size = max(1, total // parts)
    starts = [i * size for i in range(parts)]
    return [(s, (size if i < parts - 1 else total - s)) for i, s in enumerate(starts)]


def kernel(
    dims,
    table,
    base,
    cls,
    lead,
    dens1,
    dens2,
    food,
    mask_in,
    east_in,
    north_in,
    cls_row,
    out,
    sens,
    grad_out,
    wide2,
    wide1,
    done2,
    done1,
    aged2,
    aged1,
    mask_strip,
    east_strip,
    north_strip,
    rates,
    short_all,
    adem_all,
    short1,
    feed_sq,
    surv,
    grad,
    near_sum,
    far_sum,
    lsend,
    lrecv,
    zsend,
    zrecv,
    osend,
    orecv,
    z1send,
    z1recv,
    o1send,
    o1recv,
    fsend,
    frecv,
    hsend,
    hrecv,
    ssend,
    srecv,
    asend,
    arecv,
    nsend,
    nrecv,
    tsend,
    trecv,
    own_sem,
):
    tiles, group, cohorts, quarter, forage, chunks = dims
    half = group // 2
    blocks = food.shape[2]
    me = lax.axis_index("tile")
    q = lax.rem(me, group)
    first = me - q
    has_prev = me >= group
    has_next = me < tiles - group

    def peer(o):
        return first + lax.rem(q + o, group)

    def source(o):
        return lax.rem(q + group - o, group)

    barrier = pltpu.get_barrier_semaphore()
    for o in range(1, group):
        pl.semaphore_signal(barrier, inc=1, device_id={"tile": peer(o)}, device_id_type=MESH)

    spans = tiles // group
    for g in range(1, spans):
        far = lax.rem(me + g * group, tiles)
        pl.semaphore_signal(barrier, inc=1, device_id={"tile": far}, device_id_type=MESH)
    pl.semaphore_wait(barrier, group + spans - 2)

    def pref(a, k):
        return table[cls[a], k]

    def remote(src, dst, ssem, rsem, target):
        return pltpu.make_async_remote_copy(
            src_ref=src, dst_ref=dst, send_sem=ssem, recv_sem=rsem,
            device_id={"tile": target}, device_id_type=MESH,
        )

    def gather_copy(buf, ssem, rsem, o):
        return remote(buf.at[q], buf.at[q], ssem.at[o], rsem.at[o], peer(o))

    def gather_wait(buf, ssem, rsem, o):
        spot = buf.at[source(o)]
        remote(spot, spot, ssem.at[o], rsem.at[o], peer(o)).wait_recv()

    def halo(buf, lo, size, ssem, rsem, c):
        def rows(begin):
            if lo is None:
                return buf.at[pl.ds(begin, half)]
            return buf.at[pl.ds(begin, half), pl.ds(lo, size)]

        down = remote(rows(group), rows(0), ssem.at[0, c], rsem.at[0, c], me + group)
        up = remote(rows(half), rows(group + half), ssem.at[1, c], rsem.at[1, c], me - group)
        return down, up

    def halo_start(*args):
        down, up = halo(*args)

        @pl.when(has_next)
        def _():
            down.start()

        @pl.when(has_prev)
        def _():
            up.start()

    def halo_wait(*args):
        down, up = halo(*args)

        @pl.when(has_prev)
        def _():
            down.wait_recv()

        @pl.when(has_next)
        def _():
            up.wait_recv()

    def halo_sent(*args):
        down, up = halo(*args)

        @pl.when(has_next)
        def _():
            down.wait_send()

        @pl.when(has_prev)
        def _():
            up.wait_send()

    strips = ((mask_in, mask_strip), (east_in, east_strip), (north_in, north_strip))
    own_fields = [
        pltpu.make_async_copy(src, dst.at[half + q], own_sem.at[f])
        for f, (src, dst) in enumerate(strips)
    ]
    for copy in own_fields:
        copy.start()

    def field_copy(o, f):
        src, dst = strips[f]
        return remote(src, dst.at[half + q], fsend.at[o, f], frecv.at[o, f], peer(o))

    for f in range(3):
        for o in range(1, group):
            field_copy(o, f).start()

    lead_cuts = cuts(quarter + 1, chunks)
    part_cuts = cuts(quarter, chunks)
    tail = lead_cuts[-1][0]
    lead_parts = lead_cuts[:-1] + [(tail, quarter - 1 - tail), (quarter - 1, 1), (quarter, 1)]

    def lead_copy(o, p):
        lo, size = lead_parts[p]
        begin = lax.rem(q + o, group) * quarter + 1 + lo
        return remote(
            lead.at[pl.ds(jnp.minimum(begin, cohorts - size), size)],
            wide2.at[half + q, pl.ds(lo, size)],
            lsend.at[o, p], lrecv.at[o, p], peer(o),
        )

    def lead_own(p):
        lo, size = lead_parts[p]
        begin = jnp.minimum(q * quarter + 1 + lo, cohorts - size)
        return pltpu.make_async_copy(
            lead.at[pl.ds(begin, size)], wide2.at[half + q, pl.ds(lo, size)], lrecv.at[0, p]
        )

    for p in range(len(lead_parts)):
        for o in range(1, group):
            lead_copy(o, p).start()
        lead_own(p).start()

    @pl.when(jnp.logical_not(has_prev))
    def _():
        mask_strip[0:half] = jnp.zeros((half,) + mask_strip.shape[1:], jnp.int32)
        east_strip[0:half] = jnp.zeros((half,) + east_strip.shape[1:], jnp.float32)
        north_strip[0:half] = jnp.zeros((half,) + east_strip.shape[1:], jnp.float32)
        wide2[0:half] = jnp.zeros((half,) + wide2.shape[1:], jnp.float32)
        wide1[0:half] = jnp.zeros((half,) + wide1.shape[1:], jnp.float32)

    @pl.when(jnp.logical_not(has_next))
    def _():
        mask_strip[group + half :] = jnp.zeros((half,) + mask_strip.shape[1:], jnp.int32)
        east_strip[group + half :] = jnp.zeros((half,) + east_strip.shape[1:], jnp.float32)
        north_strip[group + half :] = jnp.zeros((half,) + east_strip.shape[1:], jnp.float32)
        wide2[group + half :] = jnp.zeros((half,) + wide2.shape[1:], jnp.float32)
        wide1[group + half :] = jnp.zeros((half,) + wide1.shape[1:], jnp.float32)

    zero = jnp.zeros((blocks, LANES), jnp.float32)

    def demands(dens):
        def step(a, sums):
            n = dens[a]
            return tuple(sums[k] + pref(a, k) * n for k in range(forage))

        return lax.fori_loop(0, cohorts, step, (zero,) * forage, unroll=4)

    def prepare(month, dens, short_store):
        sums = demands(dens)
        for k in range(forage):
            feed = food[month, k]
            total = feed + sums[k]
            short_store(k, sums[k] / total)
            feed_sq[month, k] = feed / (total * total)
            feed_sq[2 + month, k] = sums[k]

    def store_two(k, value):
        short_all[q, k] = value

    def store_one(k, value):
        short1[k] = value

    prepare(1, dens2, store_two)
    for o in range(1, group):
        gather_copy(short_all, ssend, srecv, o).start()

    for f, (src, dst) in enumerate(strips):
        own_fields[f].wait()
        for o in range(1, group):
            spot = dst.at[half + source(o)]
            remote(spot, spot, fsend.at[o, f], frecv.at[o, f], peer(o)).wait_recv()
        halo_start(dst, None, None, hsend, hrecv, f)
    lane = lax.broadcasted_iota(jnp.int32, (blocks, LANES), 1)
    odd = lax.rem(lax.broadcasted_iota(jnp.int32, (blocks, LANES), 0), 2) == 1
    last_lane = lane == LANES - 1
    first_lane = lane == 0

    def east_of(x):
        near = pltpu.roll(x, LANES - 1, 1)
        return jnp.where(last_lane, pltpu.roll(near, blocks - 2, 0), near)

    def west_of(x):
        near = pltpu.roll(x, 1, 1)
        return jnp.where(first_lane, pltpu.roll(near, 2, 0), near)

    def vertical(slots, s):
        above = slots[s - 1] if s > 0 and slots[s - 1] is not None else zero
        below = slots[s + 1] if s + 1 < len(slots) and slots[s + 1] is not None else zero
        north = jnp.where(odd, pltpu.roll(slots[s], 1, 0), pltpu.roll(above, blocks - 1, 0))
        south = jnp.where(odd, pltpu.roll(below, 1, 0), pltpu.roll(slots[s], blocks - 1, 0))
        return north, south

    prepare(0, dens1, store_one)

    def lead_wait(c):
        for p in [c] if c < chunks - 1 else range(c, len(lead_parts)):
            lo, size = lead_parts[p]
            for o in range(1, group):
                spot = wide2.at[half + source(o), pl.ds(lo, size)]
                remote(spot, spot, lsend.at[o, p], lrecv.at[o, p], peer(o)).wait_recv()
            lead_own(p).wait()

    lead_wait(0)
    halo_start(wide2, *lead_cuts[0], zsend, zrecv, 0)
    for f, (src, dst) in enumerate(strips):
        halo_wait(dst, None, None, hsend, hrecv, f)
    masks = [mask_strip[s].astype(jnp.float32) for s in range(2 * group)]
    for s in range(2 * group):
        mask, east, north = masks[s], east_strip[s], north_strip[s]
        mask_n, mask_s = vertical(masks, s)
        rate_n = mask * mask_n * (0.1 + jnp.maximum(north, 0.0))
        rate_s = mask * mask_s * (0.1 + jnp.maximum(-north, 0.0))
        rate_e = mask * east_of(mask) * (0.1 + jnp.maximum(east, 0.0))
        rate_w = mask * west_of(mask) * (0.1 + jnp.maximum(-east, 0.0))
        rates[s, 0] = 1.0 - rate_n - rate_s - rate_e - rate_w
        rates[s, 1] = rate_n
        rates[s, 2] = rate_s
        rates[s, 3] = rate_e
        rates[s, 4] = rate_w

    def transport(wide, done, lo, size):
        def body(i, carry):
            slots = [wide[s, i] for s in range(2 * group)]
            for step in range(SUBSTEPS):
                margin = (step + 1) // 2
                new = [None] * (2 * group)
                for s in range(margin, 2 * group - margin):
                    north, south = vertical(slots, s)
                    new[s] = (
                        rates[s, 0] * slots[s]
                        + rates[s, 1] * north
                        + rates[s, 2] * south
                        + rates[s, 3] * east_of(slots[s])
                        + rates[s, 4] * west_of(slots[s])
                    )
                slots = new
            for s in range(group):
                done[s, i] = slots[half + s]
            return carry

        lax.fori_loop(lo, lo + size, body, 0)

    def out_copy(done, aged, o, c, ssem, rsem):
        lo, size = part_cuts[c]
        return remote(
            done.at[lax.rem(q + o, group), pl.ds(lo, size)],
            aged.at[pl.ds(q * quarter + lo, size)], ssem.at[o, c], rsem.at[o, c], peer(o),
        )

    def out_own(done, aged, c, sem):
        lo, size = part_cuts[c]
        return pltpu.make_async_copy(
            done.at[q, pl.ds(lo, size)], aged.at[pl.ds(q * quarter + lo, size)], sem.at[0, c]
        )

    def out_wait(aged, o, c, ssem, rsem):
        lo, size = part_cuts[c]
        spot = aged.at[pl.ds(source(o) * quarter + lo, size)]
        remote(spot, spot, ssem.at[o, c], rsem.at[o, c], peer(o)).wait_recv()

    for c in range(chunks):
        if c + 1 < chunks:
            lead_wait(c + 1)
            halo_start(wide2, *lead_cuts[c + 1], zsend, zrecv, c + 1)
        halo_wait(wide2, *lead_cuts[c], zsend, zrecv, c)
        transport(wide2, done2, *lead_cuts[c])
        for o in range(1, group):
            out_copy(done2, aged2, o, c, osend, orecv).start()
        out_own(done2, aged2, c, orecv).start()

    def ratio_part(lo, size, aged, dens, short, sums):
        def step(a, sums):
            level = base[a]
            hunger = [pref(a, k) for k in range(forage)]
            for k in range(forage):
                level = level + hunger[k] * short[k]
            kept = jnp.exp(-level)
            surv[a] = kept
            dying = aged[a] * kept * dens[a]
            return tuple(sums[k] + hunger[k] * dying for k in range(forage))

        for part in range(group):
            start = part * quarter + lo
            sums = lax.fori_loop(start, start + size, step, sums, unroll=2)
        return sums

    def finish(month, ratio):
        adem = []
        for k in range(forage):
            adem.append(-ratio[k] * feed_sq[month, k])
            sens[month, k] = ratio[k] * feed_sq[2 + month, k] * feed_sq[month, k]
        return adem

    def slopes(aged, dens, short, adem, add):
        def step(a, carry):
            n = dens[a]
            dying = aged[a] * surv[a] * n
            for k in range(forage):
                both = n * adem[k] - dying * short[k]
                row = jnp.sum(both, axis=0, keepdims=True)
                if add:
                    row = row + grad[k, pl.ds(a, 1)]
                grad[k, pl.ds(a, 1)] = row
            return carry

        lax.fori_loop(0, cohorts, step, 0, unroll=2)

    def outgoing(aged, adem):
        def step(a, carry):
            total = aged[a] * surv[a]
            for k in range(forage):
                total = total + pref(a, k) * adem[k]
            out[a] = total
            return carry

        lax.fori_loop(0, cohorts, step, 0, unroll=4)

    short2 = [short_all[q, k] for k in range(forage)]
    ratio = (zero,) * forage
    for c in range(chunks):
        for o in range(1, group):
            out_wait(aged2, o, c, osend, orecv)
        out_own(done2, aged2, c, orecv).wait()
        ratio = ratio_part(*part_cuts[c], aged2, dens2, short2, ratio)
    adem2 = finish(1, ratio)
    for k in range(forage):
        adem_all[q, k] = adem2[k]
    for o in range(1, group):
        gather_copy(adem_all, asend, arecv, o).start()
    for o in range(1, group):
        gather_wait(short_all, ssend, srecv, o)
    for o in range(1, group):
        gather_wait(adem_all, asend, arecv, o)

    for c in range(chunks):
        lo, size = part_cuts[c]

        def middle(i, carry):
            a = jnp.minimum(q * quarter + i + 1, cohorts - 1)
            hunger = [pref(a, k) for k in range(forage)]
            for s in range(group):
                level = base[a]
                add = zero
                for k in range(forage):
                    level = level + hunger[k] * short_all[s, k]
                    add = add + hunger[k] * adem_all[s, k]
                wide1[half + s, i] = done2[s, i + 1] * jnp.exp(-level) + add
            return carry

        lax.fori_loop(lo, lo + size, middle, 0)
        halo_start(wide1, lo, size, z1send, z1recv, c)
    slopes(aged2, dens2, short2, adem2, False)

    for c in range(chunks):
        halo_wait(wide1, *part_cuts[c], z1send, z1recv, c)
        transport(wide1, done1, *part_cuts[c])
        for o in range(1, group):
            out_copy(done1, aged1, o, c, o1send, o1recv).start()
        out_own(done1, aged1, c, o1recv).start()

    short_one = [short1[k] for k in range(forage)]
    ratio = (zero,) * forage
    for c in range(chunks):
        for o in range(1, group):
            out_wait(aged1, o, c, o1send, o1recv)
        out_own(done1, aged1, c, o1recv).wait()
        ratio = ratio_part(*part_cuts[c], aged1, dens1, short_one, ratio)
    adem1 = finish(0, ratio)
    slopes(aged1, dens1, short_one, adem1, True)

    classes = table.shape[0]
    kinds = lax.broadcasted_iota(jnp.int32, (classes, cohorts), 0)
    onehot = (kinds == cls_row[...]).astype(jnp.float32)
    high = lax.Precision.HIGHEST
    by_class = jnp.concatenate(
        [
            jnp.dot(onehot, grad[k], precision=high, preferred_element_type=jnp.float32)
            for k in range(forage)
        ],
        axis=0,
    )
    ones = jnp.ones((8, LANES), jnp.float32)
    near_sum[q] = lax.dot_general(
        ones, by_class, (((1,), (1,)), ((), ())), precision=high,
        preferred_element_type=jnp.float32,
    )
    for o in range(1, group):
        gather_copy(near_sum, nsend, nrecv, o).start()
    for o in range(1, group):
        gather_wait(near_sum, nsend, nrecv, o)
    span = me // group
    far_sum[span] = sum(near_sum[i] for i in range(1, group)) + near_sum[0]

    def far_copy(g):
        far = lax.rem(me + g * group, tiles)
        return remote(far_sum.at[span], far_sum.at[span], tsend.at[g], trecv.at[g], far)

    for g in range(1, spans):
        far_copy(g).start()
    outgoing(aged1, adem1)
    for g in range(1, spans):
        spot = far_sum.at[lax.rem(span + spans - g, spans)]
        remote(spot, spot, tsend.at[g], trecv.at[g], lax.rem(me + g * group, tiles)).wait_recv()
    grad_out[...] = lax.fori_loop(
        1, spans, lambda g, total: total + far_sum[g], far_sum[0]
    ) / (tiles * blocks * LANES)
    for g in range(1, spans):
        far_copy(g).wait_send()

    for o in range(1, group):
        gather_copy(near_sum, nsend, nrecv, o).wait_send()
        for f in range(3):
            field_copy(o, f).wait_send()
        for p in range(len(lead_parts)):
            lead_copy(o, p).wait_send()
        gather_copy(short_all, ssend, srecv, o).wait_send()
        gather_copy(adem_all, asend, arecv, o).wait_send()
        for c in range(chunks):
            out_copy(done2, aged2, o, c, osend, orecv).wait_send()
            out_copy(done1, aged1, o, c, o1send, o1recv).wait_send()
    for f, (src, dst) in enumerate(strips):
        halo_sent(dst, None, None, hsend, hrecv, f)
    for c in range(chunks):
        halo_sent(wide2, *lead_cuts[c], zsend, zrecv, c)
        halo_sent(wide1, *part_cuts[c], z1send, z1recv, c)


def blocked(x):
    rows, columns = x.shape[-2:]
    head = x.shape[:-2]
    n = len(head)
    y = x.reshape(head + (rows, columns // LANES, LANES))
    y = jnp.swapaxes(y, n, n + 1)
    return y.reshape(head + (rows * columns // LANES, LANES))


def unblocked(x, rows):
    head = x.shape[:-2]
    n = len(head)
    y = x.reshape(head + (x.shape[-2] // rows, rows, LANES))
    y = jnp.swapaxes(y, n, n + 1)
    return y.reshape(head + (rows, -1))


def shards(
    final_adjoint,
    first_density,
    second_density,
    forage,
    preference,
    base_mortality,
    age_class,
    land_mask,
    east_velocity,
    north_velocity,
):
    classes, groups = preference.shape
    cohorts, rows, columns = final_adjoint.shape
    tiles = lax.axis_size("tile")
    group = 2 * SUBSTEPS // rows
    quarter = cohorts // group
    chunks = 5
    blocks = rows * columns // LANES
    f32 = jnp.float32
    dma = pltpu.SemaphoreType.DMA
    vmem = pl.BlockSpec(memory_space=pltpu.VMEM)
    smem = pl.BlockSpec(memory_space=pltpu.SMEM)
    hbm = pl.BlockSpec(memory_space=pl.ANY)
    dims = (tiles, group, cohorts, quarter, groups, chunks)
    cell = (blocks, LANES)
    pair = [dma((group, chunks)), dma((group, chunks))]
    hop = [dma((2, chunks)), dma((2, chunks))]
    one = [dma((group,)), dma((group,))]

    def body(*refs):
        kernel(dims, *refs)

    out, sens, grad = pl.pallas_call(
        body,
        out_shape=(
            jax.ShapeDtypeStruct((cohorts,) + cell, f32),
            jax.ShapeDtypeStruct((2, groups) + cell, f32),
            jax.ShapeDtypeStruct((8, groups * classes), f32),
        ),
        in_specs=[smem, smem, smem, hbm] + [vmem] * 7,
        out_specs=(vmem, vmem, vmem),
        scratch_shapes=[
            pltpu.VMEM((2 * group, quarter + 1) + cell, f32),
            pltpu.VMEM((2 * group, quarter) + cell, f32),
            pltpu.VMEM((group, quarter + 1) + cell, f32),
            pltpu.VMEM((group, quarter) + cell, f32),
            pltpu.VMEM((cohorts,) + cell, f32),
            pltpu.VMEM((cohorts,) + cell, f32),
            pltpu.VMEM((2 * group,) + cell, jnp.int32),
            pltpu.VMEM((2 * group,) + cell, f32),
            pltpu.VMEM((2 * group,) + cell, f32),
            pltpu.VMEM((2 * group, 5) + cell, f32),
            pltpu.VMEM((group, groups) + cell, f32),
            pltpu.VMEM((group, groups) + cell, f32),
            pltpu.VMEM((groups,) + cell, f32),
            pltpu.VMEM((4, groups) + cell, f32),
            pltpu.VMEM((cohorts,) + cell, f32),
            pltpu.VMEM((groups, cohorts, LANES), f32),
            pltpu.VMEM((group, 8, groups * classes), f32),
            pltpu.VMEM((tiles // group, 8, groups * classes), f32),
        ]
        + [dma((group, chunks + 2))] * 2 + hop + pair + hop + pair + [dma((group, 3))] * 2
        + [dma((2, 3))] * 2 + one + one + one + [dma((tiles // group,))] * 2 + [dma((3,))],
        compiler_params=pltpu.CompilerParams(
            collective_id=0, has_side_effects=True, vmem_limit_bytes=48 * 1024 * 1024
        ),
        name="adjoint",
    )(
        preference,
        base_mortality,
        age_class,
        blocked(final_adjoint),
        blocked(first_density),
        blocked(second_density),
        blocked(forage),
        blocked(land_mask),
        blocked(east_velocity),
        blocked(north_velocity),
        age_class.reshape(1, -1),
    )
    summed = grad[0].reshape(groups, classes).T
    return (unblocked(out, rows), unblocked(sens, rows), summed)


def solution(mesh):
    in_specs = (
        P("ens", "tile", None),
        P("ens", "tile", None),
        P("ens", "tile", None),
        P("ens", None, "tile", None),
        P("ens", None),
        P(),
        P(),
        P("tile", None),
        P("tile", None),
        P("tile", None),
    )
    out_specs = (P("ens", "tile", None), P("ens", None, "tile", None), P("ens", None))
    return jax.shard_map(shards, mesh=mesh, in_specs=in_specs, out_specs=out_specs, check_vma=False)
```

```python
import jax
import jax.numpy as jnp
from jax import lax
from jax.experimental import pallas as pl
from jax.experimental.pallas import tpu as pltpu
from jax.sharding import PartitionSpec as P

SUBSTEPS = 4
LANES = 128
MESH = pl.DeviceIdType.MESH


def cuts(total, parts):
    size = max(1, total // parts)
    starts = [i * size for i in range(parts)]
    return [(s, (size if i < parts - 1 else total - s)) for i, s in enumerate(starts)]


def kernel(
    dims,
    table,
    base,
    cls,
    lead,
    dens1_in,
    dens2_in,
    food_in,
    mask_in,
    east_in,
    north_in,
    cls_row,
    out,
    sens,
    grad_out,
    wide2,
    wide1,
    done2,
    done1,
    aged2,
    aged1,
    mask_strip,
    east_strip,
    north_strip,
    rates,
    short_all,
    adem_all,
    short1,
    feed_sq,
    dens1,
    dens2,
    food,
    surv1,
    surv2,
    decay,
    by_kind,
    living,
    adding,
    crowd,
    grad,
    by_class,
    near_sum,
    far_sum,
    lsend,
    lrecv,
    zsend,
    zrecv,
    osend,
    orecv,
    z1send,
    z1recv,
    o1send,
    o1recv,
    fsend,
    frecv,
    hsend,
    hrecv,
    ssend,
    srecv,
    asend,
    arecv,
    nsend,
    nrecv,
    tsend,
    trecv,
    own_sem,
):
    tiles, group, cohorts, quarter, forage, chunks = dims
    half = group // 2
    blocks = food.shape[2]
    classes = table.shape[1]
    me = lax.axis_index("tile")
    q = lax.rem(me, group)
    first = me - q
    has_prev = me >= group
    has_next = me < tiles - group

    def peer(o):
        return first + lax.rem(q + o, group)

    def source(o):
        return lax.rem(q + group - o, group)

    loads = [
        pltpu.make_async_copy(src, dst, own_sem.at[3 + i])
        for i, (src, dst) in enumerate(((dens2_in, dens2), (food_in, food), (dens1_in, dens1)))
    ]
    for copy in loads:
        copy.start()

    barrier = pltpu.get_barrier_semaphore()
    for o in range(1, group):
        pl.semaphore_signal(barrier, inc=1, device_id={"tile": peer(o)}, device_id_type=MESH)

    spans = tiles // group
    for g in range(1, spans):
        far = lax.rem(me + g * group, tiles)
        pl.semaphore_signal(barrier, inc=1, device_id={"tile": far}, device_id_type=MESH)
    pl.semaphore_wait(barrier, group + spans - 2)

    def pref(a, k):
        return table[k, cls[a]]

    def remote(src, dst, ssem, rsem, target):
        return pltpu.make_async_remote_copy(
            src_ref=src, dst_ref=dst, send_sem=ssem, recv_sem=rsem,
            device_id={"tile": target}, device_id_type=MESH,
        )

    def gather_copy(buf, ssem, rsem, o):
        return remote(buf.at[q], buf.at[q], ssem.at[o], rsem.at[o], peer(o))

    def gather_wait(buf, ssem, rsem, o):
        spot = buf.at[source(o)]
        remote(spot, spot, ssem.at[o], rsem.at[o], peer(o)).wait_recv()

    def halo(buf, lo, size, ssem, rsem, c):
        def rows(begin):
            if lo is None:
                return buf.at[pl.ds(begin, half)]
            return buf.at[pl.ds(begin, half), pl.ds(lo, size)]

        down = remote(rows(group), rows(0), ssem.at[0, c], rsem.at[0, c], me + group)
        up = remote(rows(half), rows(group + half), ssem.at[1, c], rsem.at[1, c], me - group)
        return down, up

    def halo_start(*args):
        down, up = halo(*args)

        @pl.when(has_next)
        def _():
            down.start()

        @pl.when(has_prev)
        def _():
            up.start()

    def halo_wait(*args):
        down, up = halo(*args)

        @pl.when(has_prev)
        def _():
            down.wait_recv()

        @pl.when(has_next)
        def _():
            up.wait_recv()

    def halo_sent(*args):
        down, up = halo(*args)

        @pl.when(has_next)
        def _():
            down.wait_send()

        @pl.when(has_prev)
        def _():
            up.wait_send()

    strips = ((mask_in, mask_strip), (east_in, east_strip), (north_in, north_strip))
    own_fields = [
        pltpu.make_async_copy(src, dst.at[half + q], own_sem.at[f])
        for f, (src, dst) in enumerate(strips)
    ]
    for copy in own_fields:
        copy.start()

    def field_copy(o, f):
        src, dst = strips[f]
        return remote(src, dst.at[half + q], fsend.at[o, f], frecv.at[o, f], peer(o))

    for f in range(3):
        for o in range(1, group):
            field_copy(o, f).start()

    lead_cuts = cuts(quarter + 1, chunks)
    part_cuts = cuts(quarter, chunks)
    tail = lead_cuts[-1][0]
    lead_parts = lead_cuts[:-1] + [(tail, quarter - 1 - tail), (quarter - 1, 1), (quarter, 1)]

    def lead_copy(o, p):
        lo, size = lead_parts[p]
        begin = lax.rem(q + o, group) * quarter + 1 + lo
        return remote(
            lead.at[pl.ds(jnp.minimum(begin, cohorts - size), size)],
            wide2.at[half + q, pl.ds(lo, size)],
            lsend.at[o, p], lrecv.at[o, p], peer(o),
        )

    def lead_own(p):
        lo, size = lead_parts[p]
        begin = jnp.minimum(q * quarter + 1 + lo, cohorts - size)
        return pltpu.make_async_copy(
            lead.at[pl.ds(begin, size)], wide2.at[half + q, pl.ds(lo, size)], lrecv.at[0, p]
        )

    for p in range(len(lead_parts)):
        for o in range(1, group):
            lead_copy(o, p).start()
        lead_own(p).start()

    @pl.when(jnp.logical_not(has_prev))
    def _():
        mask_strip[0:half] = jnp.zeros((half,) + mask_strip.shape[1:], jnp.int32)
        east_strip[0:half] = jnp.zeros((half,) + east_strip.shape[1:], jnp.float32)
        north_strip[0:half] = jnp.zeros((half,) + east_strip.shape[1:], jnp.float32)
        wide2[0:half] = jnp.zeros((half,) + wide2.shape[1:], jnp.float32)
        wide1[0:half] = jnp.zeros((half,) + wide1.shape[1:], jnp.float32)

    @pl.when(jnp.logical_not(has_next))
    def _():
        mask_strip[group + half :] = jnp.zeros((half,) + mask_strip.shape[1:], jnp.int32)
        east_strip[group + half :] = jnp.zeros((half,) + east_strip.shape[1:], jnp.float32)
        north_strip[group + half :] = jnp.zeros((half,) + east_strip.shape[1:], jnp.float32)
        wide2[group + half :] = jnp.zeros((half,) + wide2.shape[1:], jnp.float32)
        wide1[group + half :] = jnp.zeros((half,) + wide1.shape[1:], jnp.float32)

    zero = jnp.zeros((blocks, LANES), jnp.float32)

    kinds = lax.broadcasted_iota(jnp.int32, (classes, cohorts), 0)
    onehot = (kinds == cls_row[...]).astype(jnp.float32)
    high = lax.Precision.HIGHEST

    def kind_sum(values):
        return jnp.dot(onehot, values, precision=high, preferred_element_type=jnp.float32)

    def prepare(month, dens, surv, short_store):
        for r in range(blocks):
            crowd[month, :, r, :] = kind_sum(dens[:, r, :])
        shorts = []
        for k in range(forage):
            hungry = table[k, 0] * crowd[month, 0]
            for kind in range(1, classes):
                hungry = hungry + table[k, kind] * crowd[month, kind]
            feed = food[month, k]
            total = feed + hungry
            shorts.append(hungry / total)
            short_store(k, shorts[k])
            feed_sq[month, k] = feed / (total * total)
            feed_sq[2 + month, k] = hungry
        for kind in range(classes):
            by_kind[kind] = jnp.exp(-weighted(kind, shorts))

        def step(a, carry):
            surv[a] = decay[a] * by_kind[cls[a]]
            return carry

        lax.fori_loop(0, cohorts, step, 0, unroll=4)

    def weighted(kind, values):
        total = table[0, kind] * values[0]
        for k in range(1, forage):
            total = total + table[k, kind] * values[k]
        return total

    def fade(a, carry):
        decay[a] = jnp.exp(jnp.full((blocks, LANES), -base[a]))
        return carry

    lax.fori_loop(0, cohorts, fade, 0, unroll=4)

    def store_two(k, value):
        short_all[q, k] = value

    def store_one(k, value):
        short1[k] = value

    loads[0].wait()
    loads[1].wait()
    prepare(1, dens2, surv2, store_two)
    for o in range(1, group):
        gather_copy(short_all, ssend, srecv, o).start()

    for f, (src, dst) in enumerate(strips):
        own_fields[f].wait()
        for o in range(1, group):
            spot = dst.at[half + source(o)]
            remote(spot, spot, fsend.at[o, f], frecv.at[o, f], peer(o)).wait_recv()
        halo_start(dst, None, None, hsend, hrecv, f)
    lane = lax.broadcasted_iota(jnp.int32, (blocks, LANES), 1)
    odd = lax.rem(lax.broadcasted_iota(jnp.int32, (blocks, LANES), 0), 2) == 1
    last_lane = lane == LANES - 1
    first_lane = lane == 0

    def east_of(x):
        near = pltpu.roll(x, LANES - 1, 1)
        return jnp.where(last_lane, pltpu.roll(near, blocks - 2, 0), near)

    def west_of(x):
        near = pltpu.roll(x, 1, 1)
        return jnp.where(first_lane, pltpu.roll(near, 2, 0), near)

    def vertical(slots, s):
        above = slots[s - 1] if s > 0 and slots[s - 1] is not None else zero
        below = slots[s + 1] if s + 1 < len(slots) and slots[s + 1] is not None else zero
        north = jnp.where(odd, pltpu.roll(slots[s], 1, 0), pltpu.roll(above, blocks - 1, 0))
        south = jnp.where(odd, pltpu.roll(below, 1, 0), pltpu.roll(slots[s], blocks - 1, 0))
        return north, south

    loads[2].wait()
    prepare(0, dens1, surv1, store_one)

    def lead_wait(c):
        for p in [c] if c < chunks - 1 else range(c, len(lead_parts)):
            lo, size = lead_parts[p]
            for o in range(1, group):
                spot = wide2.at[half + source(o), pl.ds(lo, size)]
                remote(spot, spot, lsend.at[o, p], lrecv.at[o, p], peer(o)).wait_recv()
            lead_own(p).wait()

    lead_wait(0)
    halo_start(wide2, *lead_cuts[0], zsend, zrecv, 0)
    for f, (src, dst) in enumerate(strips):
        halo_wait(dst, None, None, hsend, hrecv, f)
    masks = [mask_strip[s].astype(jnp.float32) for s in range(2 * group)]
    for s in range(2 * group):
        mask, east, north = masks[s], east_strip[s], north_strip[s]
        mask_n, mask_s = vertical(masks, s)
        rate_n = mask * mask_n * (0.1 + jnp.maximum(north, 0.0))
        rate_s = mask * mask_s * (0.1 + jnp.maximum(-north, 0.0))
        rate_e = mask * east_of(mask) * (0.1 + jnp.maximum(east, 0.0))
        rate_w = mask * west_of(mask) * (0.1 + jnp.maximum(-east, 0.0))
        rates[s, 0] = 1.0 - rate_n - rate_s - rate_e - rate_w
        rates[s, 1] = rate_n
        rates[s, 2] = rate_s
        rates[s, 3] = rate_e
        rates[s, 4] = rate_w

    def transport(wide, done, lo, size):
        def body(i, carry):
            slots = [wide[s, i] for s in range(2 * group)]
            for step in range(SUBSTEPS):
                margin = (step + 1) // 2
                new = [None] * (2 * group)
                for s in range(margin, 2 * group - margin):
                    north, south = vertical(slots, s)
                    new[s] = (
                        rates[s, 0] * slots[s]
                        + rates[s, 1] * north
                        + rates[s, 2] * south
                        + rates[s, 3] * east_of(slots[s])
                        + rates[s, 4] * west_of(slots[s])
                    )
                slots = new
            for s in range(group):
                done[s, i] = slots[half + s]
            return carry

        lax.fori_loop(lo, lo + size, body, 0)

    def out_copy(done, aged, o, c, ssem, rsem):
        lo, size = part_cuts[c]
        return remote(
            done.at[lax.rem(q + o, group), pl.ds(lo, size)],
            aged.at[pl.ds(q * quarter + lo, size)], ssem.at[o, c], rsem.at[o, c], peer(o),
        )

    def out_own(done, aged, c, sem):
        lo, size = part_cuts[c]
        return pltpu.make_async_copy(
            done.at[q, pl.ds(lo, size)], aged.at[pl.ds(q * quarter + lo, size)], sem.at[0, c]
        )

    def out_wait(aged, o, c, ssem, rsem):
        lo, size = part_cuts[c]
        spot = aged.at[pl.ds(source(o) * quarter + lo, size)]
        remote(spot, spot, ssem.at[o, c], rsem.at[o, c], peer(o)).wait_recv()

    for c in range(chunks):
        if c + 1 < chunks:
            lead_wait(c + 1)
            halo_start(wide2, *lead_cuts[c + 1], zsend, zrecv, c + 1)
        halo_wait(wide2, *lead_cuts[c], zsend, zrecv, c)
        transport(wide2, done2, *lead_cuts[c])
        for o in range(1, group):
            out_copy(done2, aged2, o, c, osend, orecv).start()
        out_own(done2, aged2, c, orecv).start()

    def ratio_part(lo, size, aged, dens, surv, sums, short=None):
        def step(a, sums):
            dying = aged[a] * surv[a] * dens[a]
            if short is not None:
                for k in range(forage):
                    row = jnp.sum(dying * short[k], axis=0, keepdims=True)
                    grad[k, pl.ds(a, 1)] = grad[k, pl.ds(a, 1)] + row
            return tuple(sums[k] + pref(a, k) * dying for k in range(forage))

        for part in range(group):
            start = part * quarter + lo
            sums = lax.fori_loop(start, start + size, step, sums)
        return sums

    def finish(month, ratio):
        adem = []
        for k in range(forage):
            adem.append(-ratio[k] * feed_sq[month, k])
            sens[month, k] = ratio[k] * feed_sq[2 + month, k] * feed_sq[month, k]
        return adem

    def slopes(aged, dens, surv, short):
        def step(a, carry):
            dying = aged[a] * surv[a] * dens[a]
            for k in range(forage):
                grad[k, pl.ds(a, 1)] = jnp.sum(dying * short[k], axis=0, keepdims=True)
            return carry

        lax.fori_loop(0, cohorts, step, 0, unroll=2)

    def outgoing(aged, surv, lo, hi):
        def step(a, carry):
            out[a] = aged[a] * surv[a] + by_kind[cls[a]]
            return carry

        lax.fori_loop(lo, hi, step, 0, unroll=4)

    for o in range(1, group):
        gather_wait(short_all, ssend, srecv, o)
    for s in range(group):
        shorts = [short_all[s, k] for k in range(forage)]
        for kind in range(classes):
            living[kind, s] = jnp.exp(-weighted(kind, shorts))

    short2 = [short_all[q, k] for k in range(forage)]
    ratio = (zero,) * forage
    for c in range(chunks):
        for o in range(1, group):
            out_wait(aged2, o, c, osend, orecv)
        out_own(done2, aged2, c, orecv).wait()
        ratio = ratio_part(*part_cuts[c], aged2, dens2, surv2, ratio)
    adem2 = finish(1, ratio)
    for k in range(forage):
        adem_all[q, k] = adem2[k]
    for o in range(1, group):
        gather_copy(adem_all, asend, arecv, o).start()
    for o in range(1, group):
        gather_wait(adem_all, asend, arecv, o)
    for s in range(group):
        adems = [adem_all[s, k] for k in range(forage)]
        for kind in range(classes):
            adding[kind, s] = weighted(kind, adems)

    for c in range(chunks):
        lo, size = part_cuts[c]

        def middle(i, carry):
            a = jnp.minimum(q * quarter + i + 1, cohorts - 1)
            kind = cls[a]
            fading = decay[a]
            for s in range(group):
                wide1[half + s, i] = done2[s, i + 1] * (fading * living[kind, s]) + adding[kind, s]
            return carry

        lax.fori_loop(lo, lo + size, middle, 0)
        halo_start(wide1, lo, size, z1send, z1recv, c)
    slopes(aged2, dens2, surv2, short2)

    def crowd_part(month, adem):
        parts = []
        for k in range(forage):
            rows = [
                jnp.sum(crowd[month, kind] * adem[k], axis=0, keepdims=True)
                for kind in range(classes)
            ]
            parts.append(jnp.concatenate(rows, axis=0))
        return parts

    for k, part in enumerate(crowd_part(1, adem2)):
        by_class[k] = part

    for c in range(chunks):
        halo_wait(wide1, *part_cuts[c], z1send, z1recv, c)
        transport(wide1, done1, *part_cuts[c])
        for o in range(1, group):
            out_copy(done1, aged1, o, c, o1send, o1recv).start()
        out_own(done1, aged1, c, o1recv).start()

    short_one = [short1[k] for k in range(forage)]
    ratio = (zero,) * forage
    for c in range(chunks):
        for o in range(1, group):
            out_wait(aged1, o, c, o1send, o1recv)
        out_own(done1, aged1, c, o1recv).wait()
        ratio = ratio_part(*part_cuts[c], aged1, dens1, surv1, ratio, short_one)
    adem1 = finish(0, ratio)

    ones = jnp.ones((8, LANES), jnp.float32)
    parts = crowd_part(0, adem1)
    rows = []
    for k in range(forage):
        total = by_class[k] + parts[k] - kind_sum(grad[k])
        lanes_sum = lax.dot_general(
            ones, total, (((1,), (1,)), ((), ())), precision=high,
            preferred_element_type=jnp.float32,
        )
        rows.append(lanes_sum[0:1])
    near_sum[q] = jnp.concatenate(rows, axis=0)
    for o in range(1, group):
        gather_copy(near_sum, nsend, nrecv, o).start()
    for kind in range(classes):
        by_kind[kind] = weighted(kind, adem1)
    outgoing(aged1, surv1, 0, cohorts // 2)
    for o in range(1, group):
        gather_wait(near_sum, nsend, nrecv, o)
    span = me // group
    far_sum[span] = sum(near_sum[i] for i in range(1, group)) + near_sum[0]

    def far_copy(g):
        far = lax.rem(me + g * group, tiles)
        return remote(far_sum.at[span], far_sum.at[span], tsend.at[g], trecv.at[g], far)

    for g in range(1, spans):
        far_copy(g).start()
    outgoing(aged1, surv1, cohorts // 2, cohorts)
    for g in range(1, spans):
        spot = far_sum.at[lax.rem(span + spans - g, spans)]
        remote(spot, spot, tsend.at[g], trecv.at[g], lax.rem(me + g * group, tiles)).wait_recv()
    grad_out[...] = lax.fori_loop(
        1, spans, lambda g, total: total + far_sum[g], far_sum[0]
    ) / (tiles * blocks * LANES)
    for g in range(1, spans):
        far_copy(g).wait_send()

    for o in range(1, group):
        gather_copy(near_sum, nsend, nrecv, o).wait_send()
        for f in range(3):
            field_copy(o, f).wait_send()
        for p in range(len(lead_parts)):
            lead_copy(o, p).wait_send()
        gather_copy(short_all, ssend, srecv, o).wait_send()
        gather_copy(adem_all, asend, arecv, o).wait_send()
        for c in range(chunks):
            out_copy(done2, aged2, o, c, osend, orecv).wait_send()
            out_copy(done1, aged1, o, c, o1send, o1recv).wait_send()
    for f, (src, dst) in enumerate(strips):
        halo_sent(dst, None, None, hsend, hrecv, f)
    for c in range(chunks):
        halo_sent(wide2, *lead_cuts[c], zsend, zrecv, c)
        halo_sent(wide1, *part_cuts[c], z1send, z1recv, c)


def blocked(x):
    rows, columns = x.shape[-2:]
    head = x.shape[:-2]
    n = len(head)
    y = x.reshape(head + (rows, columns // LANES, LANES))
    y = jnp.swapaxes(y, n, n + 1)
    return y.reshape(head + (rows * columns // LANES, LANES))


def unblocked(x, rows):
    head = x.shape[:-2]
    n = len(head)
    y = x.reshape(head + (x.shape[-2] // rows, rows, LANES))
    y = jnp.swapaxes(y, n, n + 1)
    return y.reshape(head + (rows, -1))


def shards(
    final_adjoint,
    first_density,
    second_density,
    forage,
    preference,
    base_mortality,
    age_class,
    land_mask,
    east_velocity,
    north_velocity,
):
    classes, groups = preference.shape
    cohorts, rows, columns = final_adjoint.shape
    tiles = lax.axis_size("tile")
    group = 2 * SUBSTEPS // rows
    quarter = cohorts // group
    chunks = 8
    blocks = rows * columns // LANES
    f32 = jnp.float32
    dma = pltpu.SemaphoreType.DMA
    vmem = pl.BlockSpec(memory_space=pltpu.VMEM)
    smem = pl.BlockSpec(memory_space=pltpu.SMEM)
    hbm = pl.BlockSpec(memory_space=pl.ANY)
    dims = (tiles, group, cohorts, quarter, groups, chunks)
    cell = (blocks, LANES)
    pair = [dma((group, chunks)), dma((group, chunks))]
    hop = [dma((2, chunks)), dma((2, chunks))]
    one = [dma((group,)), dma((group,))]

    def body(*refs):
        kernel(dims, *refs)

    out, sens, grad = pl.pallas_call(
        body,
        out_shape=(
            jax.ShapeDtypeStruct((cohorts,) + cell, f32),
            jax.ShapeDtypeStruct((2, groups) + cell, f32),
            jax.ShapeDtypeStruct((groups, classes), f32),
        ),
        in_specs=[smem, smem, smem] + [hbm] * 7 + [vmem],
        out_specs=(vmem, vmem, vmem),
        scratch_shapes=[
            pltpu.VMEM((2 * group, quarter + 1) + cell, f32),
            pltpu.VMEM((2 * group, quarter) + cell, f32),
            pltpu.VMEM((group, quarter + 1) + cell, f32),
            pltpu.VMEM((group, quarter) + cell, f32),
            pltpu.VMEM((cohorts,) + cell, f32),
            pltpu.VMEM((cohorts,) + cell, f32),
            pltpu.VMEM((2 * group,) + cell, jnp.int32),
            pltpu.VMEM((2 * group,) + cell, f32),
            pltpu.VMEM((2 * group,) + cell, f32),
            pltpu.VMEM((2 * group, 5) + cell, f32),
            pltpu.VMEM((group, groups) + cell, f32),
            pltpu.VMEM((group, groups) + cell, f32),
            pltpu.VMEM((groups,) + cell, f32),
            pltpu.VMEM((4, groups) + cell, f32),
            pltpu.VMEM((cohorts,) + cell, f32),
            pltpu.VMEM((cohorts,) + cell, f32),
            pltpu.VMEM((2, groups) + cell, f32),
            pltpu.VMEM((cohorts,) + cell, f32),
            pltpu.VMEM((cohorts,) + cell, f32),
            pltpu.VMEM((cohorts,) + cell, f32),
            pltpu.VMEM((classes,) + cell, f32),
            pltpu.VMEM((classes, group) + cell, f32),
            pltpu.VMEM((classes, group) + cell, f32),
            pltpu.VMEM((2, classes) + cell, f32),
            pltpu.VMEM((groups, cohorts, LANES), f32),
            pltpu.VMEM((groups, classes, LANES), f32),
            pltpu.VMEM((group, groups, classes), f32),
            pltpu.VMEM((tiles // group, groups, classes), f32),
        ]
        + [dma((group, chunks + 2))] * 2 + hop + pair + hop + pair + [dma((group, 3))] * 2
        + [dma((2, 3))] * 2 + one + one + one + [dma((tiles // group,))] * 2 + [dma((6,))],
        compiler_params=pltpu.CompilerParams(
            collective_id=0, has_side_effects=True, vmem_limit_bytes=60 * 1024 * 1024
        ),
        name="adjoint",
    )(
        preference.T,
        base_mortality,
        age_class,
        blocked(final_adjoint),
        blocked(first_density),
        blocked(second_density),
        blocked(forage),
        blocked(land_mask),
        blocked(east_velocity),
        blocked(north_velocity),
        age_class.reshape(1, -1),
    )
    summed = grad.T
    return (unblocked(out, rows), unblocked(sens, rows), summed)


def solution(mesh):
    in_specs = (
        P("ens", "tile", None),
        P("ens", "tile", None),
        P("ens", "tile", None),
        P("ens", None, "tile", None),
        P("ens", None),
        P(),
        P(),
        P("tile", None),
        P("tile", None),
        P("tile", None),
    )
    out_specs = (P("ens", "tile", None), P("ens", None, "tile", None), P("ens", None))
    return jax.shard_map(shards, mesh=mesh, in_specs=in_specs, out_specs=out_specs, check_vma=False)
```

```python
import jax
import jax.numpy as jnp
from jax import lax
from jax.experimental import pallas as pl
from jax.experimental.pallas import tpu as pltpu
from jax.sharding import PartitionSpec as P

SUBSTEPS = 4
LANES = 128
MESH = pl.DeviceIdType.MESH


def cuts(total, parts):
    size = max(1, total // parts)
    starts = [i * size for i in range(parts)]
    return [(s, (size if i < parts - 1 else total - s)) for i, s in enumerate(starts)]


def kernel(
    dims,
    table,
    base,
    cls,
    lead,
    dens1_in,
    dens2_in,
    food_in,
    mask_in,
    east_in,
    north_in,
    cls_row,
    out,
    sens,
    grad_out,
    wide2,
    wide1,
    done2,
    done1,
    aged2,
    aged1,
    mask_strip,
    east_strip,
    north_strip,
    rates,
    short_all,
    adem_all,
    short1,
    feed_sq,
    dens1,
    dens2,
    food,
    surv1,
    surv2,
    decay,
    by_kind,
    living,
    adding,
    crowd,
    grad,
    by_class,
    near_sum,
    far_sum,
    lsend,
    lrecv,
    zsend,
    zrecv,
    osend,
    orecv,
    z1send,
    z1recv,
    o1send,
    o1recv,
    fsend,
    frecv,
    hsend,
    hrecv,
    ssend,
    srecv,
    asend,
    arecv,
    nsend,
    nrecv,
    tsend,
    trecv,
    own_sem,
):
    tiles, group, cohorts, quarter, forage, chunks = dims
    half = group // 2
    blocks = food.shape[2]
    classes = table.shape[1]
    me = lax.axis_index("tile")
    q = lax.rem(me, group)
    first = me - q
    has_prev = me >= group
    has_next = me < tiles - group

    def peer(o):
        return first + lax.rem(q + o, group)

    def source(o):
        return lax.rem(q + group - o, group)

    loads = [
        pltpu.make_async_copy(src, dst, own_sem.at[3 + i])
        for i, (src, dst) in enumerate(((dens2_in, dens2), (food_in, food), (dens1_in, dens1)))
    ]
    for copy in loads:
        copy.start()

    barrier = pltpu.get_barrier_semaphore()
    for o in range(1, group):
        pl.semaphore_signal(barrier, inc=1, device_id={"tile": peer(o)}, device_id_type=MESH)

    spans = tiles // group
    for g in range(1, spans):
        far = lax.rem(me + g * group, tiles)
        pl.semaphore_signal(barrier, inc=1, device_id={"tile": far}, device_id_type=MESH)
    pl.semaphore_wait(barrier, group + spans - 2)

    def pref(a, k):
        return table[k, cls[a]]

    def remote(src, dst, ssem, rsem, target):
        return pltpu.make_async_remote_copy(
            src_ref=src, dst_ref=dst, send_sem=ssem, recv_sem=rsem,
            device_id={"tile": target}, device_id_type=MESH,
        )

    def gather_copy(buf, ssem, rsem, o):
        return remote(buf.at[q], buf.at[q], ssem.at[o], rsem.at[o], peer(o))

    def gather_wait(buf, ssem, rsem, o):
        spot = buf.at[source(o)]
        remote(spot, spot, ssem.at[o], rsem.at[o], peer(o)).wait_recv()

    def halo(buf, lo, size, ssem, rsem, c):
        def rows(begin):
            if lo is None:
                return buf.at[pl.ds(begin, half)]
            return buf.at[pl.ds(begin, half), pl.ds(lo, size)]

        down = remote(rows(group), rows(0), ssem.at[0, c], rsem.at[0, c], me + group)
        up = remote(rows(half), rows(group + half), ssem.at[1, c], rsem.at[1, c], me - group)
        return down, up

    def halo_start(*args):
        down, up = halo(*args)

        @pl.when(has_next)
        def _():
            down.start()

        @pl.when(has_prev)
        def _():
            up.start()

    def halo_wait(*args):
        down, up = halo(*args)

        @pl.when(has_prev)
        def _():
            down.wait_recv()

        @pl.when(has_next)
        def _():
            up.wait_recv()

    def halo_sent(*args):
        down, up = halo(*args)

        @pl.when(has_next)
        def _():
            down.wait_send()

        @pl.when(has_prev)
        def _():
            up.wait_send()

    strips = ((mask_in, mask_strip), (east_in, east_strip), (north_in, north_strip))
    own_fields = [
        pltpu.make_async_copy(src, dst.at[half + q], own_sem.at[f])
        for f, (src, dst) in enumerate(strips)
    ]
    for copy in own_fields:
        copy.start()

    def field_copy(o, f):
        src, dst = strips[f]
        return remote(src, dst.at[half + q], fsend.at[o, f], frecv.at[o, f], peer(o))

    for f in range(3):
        for o in range(1, group):
            field_copy(o, f).start()

    lead_cuts = cuts(quarter + 1, chunks)
    part_cuts = cuts(quarter, chunks)
    tail = lead_cuts[-1][0]
    lead_parts = lead_cuts[:-1] + [(tail, quarter - 1 - tail), (quarter - 1, 1), (quarter, 1)]

    def lead_copy(o, p):
        lo, size = lead_parts[p]
        begin = lax.rem(q + o, group) * quarter + 1 + lo
        return remote(
            lead.at[pl.ds(jnp.minimum(begin, cohorts - size), size)],
            wide2.at[half + q, pl.ds(lo, size)],
            lsend.at[o, p], lrecv.at[o, p], peer(o),
        )

    def lead_own(p):
        lo, size = lead_parts[p]
        begin = jnp.minimum(q * quarter + 1 + lo, cohorts - size)
        return pltpu.make_async_copy(
            lead.at[pl.ds(begin, size)], wide2.at[half + q, pl.ds(lo, size)], lrecv.at[0, p]
        )

    for p in range(len(lead_parts)):
        for o in range(1, group):
            lead_copy(o, p).start()
        lead_own(p).start()

    @pl.when(jnp.logical_not(has_prev))
    def _():
        mask_strip[0:half] = jnp.zeros((half,) + mask_strip.shape[1:], jnp.int32)
        east_strip[0:half] = jnp.zeros((half,) + east_strip.shape[1:], jnp.float32)
        north_strip[0:half] = jnp.zeros((half,) + east_strip.shape[1:], jnp.float32)
        wide2[0:half] = jnp.zeros((half,) + wide2.shape[1:], jnp.float32)
        wide1[0:half] = jnp.zeros((half,) + wide1.shape[1:], jnp.float32)

    @pl.when(jnp.logical_not(has_next))
    def _():
        mask_strip[group + half :] = jnp.zeros((half,) + mask_strip.shape[1:], jnp.int32)
        east_strip[group + half :] = jnp.zeros((half,) + east_strip.shape[1:], jnp.float32)
        north_strip[group + half :] = jnp.zeros((half,) + east_strip.shape[1:], jnp.float32)
        wide2[group + half :] = jnp.zeros((half,) + wide2.shape[1:], jnp.float32)
        wide1[group + half :] = jnp.zeros((half,) + wide1.shape[1:], jnp.float32)

    zero = jnp.zeros((blocks, LANES), jnp.float32)

    kinds = lax.broadcasted_iota(jnp.int32, (classes, cohorts), 0)
    onehot = (kinds == cls_row[...]).astype(jnp.float32)
    high = lax.Precision.HIGHEST

    def kind_sum(values):
        return jnp.dot(onehot, values, precision=high, preferred_element_type=jnp.float32)

    def prepare(month, dens, surv, short_store):
        for r in range(blocks):
            crowd[month, :, r, :] = kind_sum(dens[:, r, :])
        shorts = []
        for k in range(forage):
            hungry = table[k, 0] * crowd[month, 0]
            for kind in range(1, classes):
                hungry = hungry + table[k, kind] * crowd[month, kind]
            feed = food[month, k]
            total = feed + hungry
            shorts.append(hungry / total)
            short_store(k, shorts[k])
            feed_sq[month, k] = feed / (total * total)
            feed_sq[2 + month, k] = hungry
        for kind in range(classes):
            by_kind[kind] = jnp.exp(-weighted(kind, shorts))

        def step(a, carry):
            surv[a] = decay[a] * by_kind[cls[a]]
            return carry

        lax.fori_loop(0, cohorts, step, 0, unroll=4)

    def weighted(kind, values):
        total = table[0, kind] * values[0]
        for k in range(1, forage):
            total = total + table[k, kind] * values[k]
        return total

    def fade(a, carry):
        decay[a] = jnp.exp(jnp.full((blocks, LANES), -base[a]))
        return carry


    def store_two(k, value):
        short_all[q, k] = value

    def store_one(k, value):
        short1[k] = value


    for f, (src, dst) in enumerate(strips):
        own_fields[f].wait()
        for o in range(1, group):
            spot = dst.at[half + source(o)]
            remote(spot, spot, fsend.at[o, f], frecv.at[o, f], peer(o)).wait_recv()
        halo_start(dst, None, None, hsend, hrecv, f)
    lane = lax.broadcasted_iota(jnp.int32, (blocks, LANES), 1)
    odd = lax.rem(lax.broadcasted_iota(jnp.int32, (blocks, LANES), 0), 2) == 1
    last_lane = lane == LANES - 1
    first_lane = lane == 0

    def east_of(x):
        near = pltpu.roll(x, LANES - 1, 1)
        return jnp.where(last_lane, pltpu.roll(near, blocks - 2, 0), near)

    def west_of(x):
        near = pltpu.roll(x, 1, 1)
        return jnp.where(first_lane, pltpu.roll(near, 2, 0), near)

    def vertical(slots, s):
        above = slots[s - 1] if s > 0 and slots[s - 1] is not None else zero
        below = slots[s + 1] if s + 1 < len(slots) and slots[s + 1] is not None else zero
        north = jnp.where(odd, pltpu.roll(slots[s], 1, 0), pltpu.roll(above, blocks - 1, 0))
        south = jnp.where(odd, pltpu.roll(below, 1, 0), pltpu.roll(slots[s], blocks - 1, 0))
        return north, south


    def lead_wait(c):
        for p in [c] if c < chunks - 1 else range(c, len(lead_parts)):
            lo, size = lead_parts[p]
            for o in range(1, group):
                spot = wide2.at[half + source(o), pl.ds(lo, size)]
                remote(spot, spot, lsend.at[o, p], lrecv.at[o, p], peer(o)).wait_recv()
            lead_own(p).wait()

    lead_wait(0)
    halo_start(wide2, *lead_cuts[0], zsend, zrecv, 0)
    for f, (src, dst) in enumerate(strips):
        halo_wait(dst, None, None, hsend, hrecv, f)
    masks = [mask_strip[s].astype(jnp.float32) for s in range(2 * group)]
    for s in range(2 * group):
        mask, east, north = masks[s], east_strip[s], north_strip[s]
        mask_n, mask_s = vertical(masks, s)
        rate_n = mask * mask_n * (0.1 + jnp.maximum(north, 0.0))
        rate_s = mask * mask_s * (0.1 + jnp.maximum(-north, 0.0))
        rate_e = mask * east_of(mask) * (0.1 + jnp.maximum(east, 0.0))
        rate_w = mask * west_of(mask) * (0.1 + jnp.maximum(-east, 0.0))
        rates[s, 0] = 1.0 - rate_n - rate_s - rate_e - rate_w
        rates[s, 1] = rate_n
        rates[s, 2] = rate_s
        rates[s, 3] = rate_e
        rates[s, 4] = rate_w

    def transport(wide, done, lo, size):
        def body(i, carry):
            slots = [wide[s, i] for s in range(2 * group)]
            for step in range(SUBSTEPS):
                margin = (step + 1) // 2
                new = [None] * (2 * group)
                for s in range(margin, 2 * group - margin):
                    north, south = vertical(slots, s)
                    new[s] = (
                        rates[s, 0] * slots[s]
                        + rates[s, 1] * north
                        + rates[s, 2] * south
                        + rates[s, 3] * east_of(slots[s])
                        + rates[s, 4] * west_of(slots[s])
                    )
                slots = new
            for s in range(group):
                done[s, i] = slots[half + s]
            return carry

        lax.fori_loop(lo, lo + size, body, 0)

    def out_copy(done, aged, o, c, ssem, rsem):
        lo, size = part_cuts[c]
        return remote(
            done.at[lax.rem(q + o, group), pl.ds(lo, size)],
            aged.at[pl.ds(q * quarter + lo, size)], ssem.at[o, c], rsem.at[o, c], peer(o),
        )

    def out_own(done, aged, c, sem):
        lo, size = part_cuts[c]
        return pltpu.make_async_copy(
            done.at[q, pl.ds(lo, size)], aged.at[pl.ds(q * quarter + lo, size)], sem.at[0, c]
        )

    def out_wait(aged, o, c, ssem, rsem):
        lo, size = part_cuts[c]
        spot = aged.at[pl.ds(source(o) * quarter + lo, size)]
        remote(spot, spot, ssem.at[o, c], rsem.at[o, c], peer(o)).wait_recv()

    for c in range(chunks):
        if c + 1 < chunks:
            lead_wait(c + 1)
            halo_start(wide2, *lead_cuts[c + 1], zsend, zrecv, c + 1)
        if c + 2 == chunks:
            lax.fori_loop(0, cohorts, fade, 0, unroll=4)
            loads[0].wait()
            loads[1].wait()
            prepare(1, dens2, surv2, store_two)
            for o in range(1, group):
                gather_copy(short_all, ssend, srecv, o).start()
        halo_wait(wide2, *lead_cuts[c], zsend, zrecv, c)
        transport(wide2, done2, *lead_cuts[c])
        for o in range(1, group):
            out_copy(done2, aged2, o, c, osend, orecv).start()
        out_own(done2, aged2, c, orecv).start()

    loads[2].wait()
    prepare(0, dens1, surv1, store_one)

    def ratio_part(lo, size, aged, dens, surv, sums, short=None):
        def step(a, sums):
            dying = aged[a] * surv[a] * dens[a]
            if short is not None:
                for k in range(forage):
                    row = jnp.sum(dying * short[k], axis=0, keepdims=True)
                    grad[k, pl.ds(a, 1)] = grad[k, pl.ds(a, 1)] + row
            return tuple(sums[k] + pref(a, k) * dying for k in range(forage))

        for part in range(group):
            start = part * quarter + lo
            sums = lax.fori_loop(start, start + size, step, sums)
        return sums

    def finish(month, ratio):
        adem = []
        for k in range(forage):
            adem.append(-ratio[k] * feed_sq[month, k])
            sens[month, k] = ratio[k] * feed_sq[2 + month, k] * feed_sq[month, k]
        return adem

    def slopes(aged, dens, surv, short):
        def step(a, carry):
            dying = aged[a] * surv[a] * dens[a]
            for k in range(forage):
                grad[k, pl.ds(a, 1)] = jnp.sum(dying * short[k], axis=0, keepdims=True)
            return carry

        lax.fori_loop(0, cohorts, step, 0, unroll=2)

    def outgoing(aged, surv, lo, hi):
        def step(a, carry):
            out[a] = aged[a] * surv[a] + by_kind[cls[a]]
            return carry

        lax.fori_loop(lo, hi, step, 0, unroll=4)

    for o in range(1, group):
        gather_wait(short_all, ssend, srecv, o)
    for s in range(group):
        shorts = [short_all[s, k] for k in range(forage)]
        for kind in range(classes):
            living[kind, s] = jnp.exp(-weighted(kind, shorts))

    short2 = [short_all[q, k] for k in range(forage)]
    ratio = (zero,) * forage
    for c in range(chunks):
        for o in range(1, group):
            out_wait(aged2, o, c, osend, orecv)
        out_own(done2, aged2, c, orecv).wait()
        ratio = ratio_part(*part_cuts[c], aged2, dens2, surv2, ratio)
    adem2 = finish(1, ratio)
    for k in range(forage):
        adem_all[q, k] = adem2[k]
    for o in range(1, group):
        gather_copy(adem_all, asend, arecv, o).start()
    for o in range(1, group):
        gather_wait(adem_all, asend, arecv, o)
    for s in range(group):
        adems = [adem_all[s, k] for k in range(forage)]
        for kind in range(classes):
            adding[kind, s] = weighted(kind, adems)

    for c in range(chunks):
        lo, size = part_cuts[c]

        def middle(i, carry):
            a = jnp.minimum(q * quarter + i + 1, cohorts - 1)
            kind = cls[a]
            fading = decay[a]
            for s in range(group):
                wide1[half + s, i] = done2[s, i + 1] * (fading * living[kind, s]) + adding[kind, s]
            return carry

        lax.fori_loop(lo, lo + size, middle, 0)
        halo_start(wide1, lo, size, z1send, z1recv, c)
    slopes(aged2, dens2, surv2, short2)

    def crowd_part(month, adem):
        parts = []
        for k in range(forage):
            rows = [
                jnp.sum(crowd[month, kind] * adem[k], axis=0, keepdims=True)
                for kind in range(classes)
            ]
            parts.append(jnp.concatenate(rows, axis=0))
        return parts

    for k, part in enumerate(crowd_part(1, adem2)):
        by_class[k] = part

    for c in range(chunks):
        halo_wait(wide1, *part_cuts[c], z1send, z1recv, c)
        transport(wide1, done1, *part_cuts[c])
        for o in range(1, group):
            out_copy(done1, aged1, o, c, o1send, o1recv).start()
        out_own(done1, aged1, c, o1recv).start()

    short_one = [short1[k] for k in range(forage)]
    ratio = (zero,) * forage
    for c in range(chunks):
        for o in range(1, group):
            out_wait(aged1, o, c, o1send, o1recv)
        out_own(done1, aged1, c, o1recv).wait()
        ratio = ratio_part(*part_cuts[c], aged1, dens1, surv1, ratio, short_one)
    adem1 = finish(0, ratio)

    ones = jnp.ones((8, LANES), jnp.float32)
    parts = crowd_part(0, adem1)
    rows = []
    for k in range(forage):
        total = by_class[k] + parts[k] - kind_sum(grad[k])
        lanes_sum = lax.dot_general(
            ones, total, (((1,), (1,)), ((), ())), precision=high,
            preferred_element_type=jnp.float32,
        )
        rows.append(lanes_sum[0:1])
    near_sum[q] = jnp.concatenate(rows, axis=0)
    for o in range(1, group):
        gather_copy(near_sum, nsend, nrecv, o).start()
    for kind in range(classes):
        by_kind[kind] = weighted(kind, adem1)
    outgoing(aged1, surv1, 0, cohorts // 2)
    for o in range(1, group):
        gather_wait(near_sum, nsend, nrecv, o)
    span = me // group
    far_sum[span] = sum(near_sum[i] for i in range(1, group)) + near_sum[0]

    def far_copy(g):
        far = lax.rem(me + g * group, tiles)
        return remote(far_sum.at[span], far_sum.at[span], tsend.at[g], trecv.at[g], far)

    for g in range(1, spans):
        far_copy(g).start()
    outgoing(aged1, surv1, cohorts // 2, cohorts)
    for g in range(1, spans):
        spot = far_sum.at[lax.rem(span + spans - g, spans)]
        remote(spot, spot, tsend.at[g], trecv.at[g], lax.rem(me + g * group, tiles)).wait_recv()
    grad_out[...] = lax.fori_loop(
        1, spans, lambda g, total: total + far_sum[g], far_sum[0]
    ) / (tiles * blocks * LANES)
    for g in range(1, spans):
        far_copy(g).wait_send()

    for o in range(1, group):
        gather_copy(near_sum, nsend, nrecv, o).wait_send()
        for f in range(3):
            field_copy(o, f).wait_send()
        for p in range(len(lead_parts)):
            lead_copy(o, p).wait_send()
        gather_copy(short_all, ssend, srecv, o).wait_send()
        gather_copy(adem_all, asend, arecv, o).wait_send()
        for c in range(chunks):
            out_copy(done2, aged2, o, c, osend, orecv).wait_send()
            out_copy(done1, aged1, o, c, o1send, o1recv).wait_send()
    for f, (src, dst) in enumerate(strips):
        halo_sent(dst, None, None, hsend, hrecv, f)
    for c in range(chunks):
        halo_sent(wide2, *lead_cuts[c], zsend, zrecv, c)
        halo_sent(wide1, *part_cuts[c], z1send, z1recv, c)


def blocked(x):
    rows, columns = x.shape[-2:]
    head = x.shape[:-2]
    n = len(head)
    y = x.reshape(head + (rows, columns // LANES, LANES))
    y = jnp.swapaxes(y, n, n + 1)
    return y.reshape(head + (rows * columns // LANES, LANES))


def unblocked(x, rows):
    head = x.shape[:-2]
    n = len(head)
    y = x.reshape(head + (x.shape[-2] // rows, rows, LANES))
    y = jnp.swapaxes(y, n, n + 1)
    return y.reshape(head + (rows, -1))


def shards(
    final_adjoint,
    first_density,
    second_density,
    forage,
    preference,
    base_mortality,
    age_class,
    land_mask,
    east_velocity,
    north_velocity,
):
    classes, groups = preference.shape
    cohorts, rows, columns = final_adjoint.shape
    tiles = lax.axis_size("tile")
    group = 2 * SUBSTEPS // rows
    quarter = cohorts // group
    chunks = 8
    blocks = rows * columns // LANES
    f32 = jnp.float32
    dma = pltpu.SemaphoreType.DMA
    vmem = pl.BlockSpec(memory_space=pltpu.VMEM)
    smem = pl.BlockSpec(memory_space=pltpu.SMEM)
    hbm = pl.BlockSpec(memory_space=pl.ANY)
    dims = (tiles, group, cohorts, quarter, groups, chunks)
    cell = (blocks, LANES)
    pair = [dma((group, chunks)), dma((group, chunks))]
    hop = [dma((2, chunks)), dma((2, chunks))]
    one = [dma((group,)), dma((group,))]

    def body(*refs):
        kernel(dims, *refs)

    out, sens, grad = pl.pallas_call(
        body,
        out_shape=(
            jax.ShapeDtypeStruct((cohorts,) + cell, f32),
            jax.ShapeDtypeStruct((2, groups) + cell, f32),
            jax.ShapeDtypeStruct((groups, classes), f32),
        ),
        in_specs=[smem, smem, smem] + [hbm] * 7 + [vmem],
        out_specs=(vmem, vmem, vmem),
        scratch_shapes=[
            pltpu.VMEM((2 * group, quarter + 1) + cell, f32),
            pltpu.VMEM((2 * group, quarter) + cell, f32),
            pltpu.VMEM((group, quarter + 1) + cell, f32),
            pltpu.VMEM((group, quarter) + cell, f32),
            pltpu.VMEM((cohorts,) + cell, f32),
            pltpu.VMEM((cohorts,) + cell, f32),
            pltpu.VMEM((2 * group,) + cell, jnp.int32),
            pltpu.VMEM((2 * group,) + cell, f32),
            pltpu.VMEM((2 * group,) + cell, f32),
            pltpu.VMEM((2 * group, 5) + cell, f32),
            pltpu.VMEM((group, groups) + cell, f32),
            pltpu.VMEM((group, groups) + cell, f32),
            pltpu.VMEM((groups,) + cell, f32),
            pltpu.VMEM((4, groups) + cell, f32),
            pltpu.VMEM((cohorts,) + cell, f32),
            pltpu.VMEM((cohorts,) + cell, f32),
            pltpu.VMEM((2, groups) + cell, f32),
            pltpu.VMEM((cohorts,) + cell, f32),
            pltpu.VMEM((cohorts,) + cell, f32),
            pltpu.VMEM((cohorts,) + cell, f32),
            pltpu.VMEM((classes,) + cell, f32),
            pltpu.VMEM((classes, group) + cell, f32),
            pltpu.VMEM((classes, group) + cell, f32),
            pltpu.VMEM((2, classes) + cell, f32),
            pltpu.VMEM((groups, cohorts, LANES), f32),
            pltpu.VMEM((groups, classes, LANES), f32),
            pltpu.VMEM((group, groups, classes), f32),
            pltpu.VMEM((tiles // group, groups, classes), f32),
        ]
        + [dma((group, chunks + 2))] * 2 + hop + pair + hop + pair + [dma((group, 3))] * 2
        + [dma((2, 3))] * 2 + one + one + one + [dma((tiles // group,))] * 2 + [dma((6,))],
        compiler_params=pltpu.CompilerParams(
            collective_id=0, has_side_effects=True, vmem_limit_bytes=60 * 1024 * 1024
        ),
        name="adjoint",
    )(
        preference.T,
        base_mortality,
        age_class,
        blocked(final_adjoint),
        blocked(first_density),
        blocked(second_density),
        blocked(forage),
        blocked(land_mask),
        blocked(east_velocity),
        blocked(north_velocity),
        age_class.reshape(1, -1),
    )
    summed = grad.T
    return (unblocked(out, rows), unblocked(sens, rows), summed)


def solution(mesh):
    in_specs = (
        P("ens", "tile", None),
        P("ens", "tile", None),
        P("ens", "tile", None),
        P("ens", None, "tile", None),
        P("ens", None),
        P(),
        P(),
        P("tile", None),
        P("tile", None),
        P("tile", None),
    )
    out_specs = (P("ens", "tile", None), P("ens", None, "tile", None), P("ens", None))
    return jax.shard_map(shards, mesh=mesh, in_specs=in_specs, out_specs=out_specs, check_vma=False)
```
